128 devices in a mesh: row: 32 (over x_hi, z, y), ch: 4 (over x_lo, core).
Axes of the slice: x: 4 (x_hi: 2, x_lo: 2; x = x_hi * 2 + x_lo), y: 4, z: 4, core: 2. Of those that a mesh axis runs over, the one named last changes fastest.
Arguments:
- pair_rep: float32 [256, 256, 128], P(('row', 'ch')), may hold values from -6 to 6
- pair_mask: int32 [256, 256], P(('row', 'ch')), may hold values from 0 to 1, as said below
- ln_in_gain: float32 [128], replicated, may hold values from 0.5 to 1.5
- ln_in_bias: float32 [128], replicated, may hold values from -3 to 3
- w_in: float32 [128, 640], replicated, may hold values from -0.5 to 0.5
- b_in: float32 [640], replicated, may hold values from -3 to 3
- ln_out_gain: float32 [128], replicated, may hold values from 0.5 to 1.5
- ln_out_bias: float32 [128], replicated, may hold values from -3 to 3
- w_out: float32 [128, 128], replicated, may hold values from -0.5 to 0.5
- b_out: float32 [128], replicated, may hold values from -3 to 3
- cotangent: float32 [256, 256, 128], P(('row', 'ch')), may hold values from -6 to 6
Outputs:
- update: float32 [256, 256, 128], P(('row', 'ch'))
- grad_pair: float32 [256, 256, 128], P(('row', 'ch'))
- grad_w_in: float32 [128, 640], replicated
- grad_w_out: float32 [128, 128], replicated
The draws below stay inside these ranges and needn't reach their ends.
Inputs may be any that keep to these rules, and one draw needn't show every extreme that they name: pair_mask[i, k] = m_i m_k, where m is 1 for the residues present in the crop and 0 otherwise.
All inputs are finite; a program needn't handle non-finite values.
Results may differ from the reference program's by a relative error of at most 0.00009.
Values sent between devices are 32-bit elements; how exact they have to be, the bound alone decides.
No kernel may reach another device: no remote copies, remote signals or barrier semaphores. Data moves between devices by JAX's collectives and lax.ppermute only.
A program may use at most 64 MiB of HBM per device.

```python
import jax
import jax.numpy as jnp
from jax import lax

C = 128
H = 128
N = 256
N_ROW = 32
N_CH = 4


def draw_pair_mask(key, part):
    residue = jax.random.randint(key, (N,), 0, 8)
    present = (residue > 0).astype(jnp.int32)
    return present[:, None] * present[None, :]


def block_scale(rng, extent, cuts, low, top_value):
    def one(axis_at, parts):
        draws = jax.random.uniform(jax.random.fold_in(jax.random.fold_in(rng, 6), axis_at), (parts,), jnp.float32, low / len(cuts), top_value / len(cuts))
        return jnp.repeat(jnp.exp(draws), extent[axis_at] // parts).reshape((-1,) + (1,) * (len(extent) - axis_at - 1))

    gain = one(*cuts[0])
    for cut in cuts[1:]:
        gain = gain * one(*cut)
    return gain


def scatter_about(key, extent, scale, most, split=(), kind=jnp.bfloat16):
    factor_of = block_scale(key, extent, split, -0.22, 0.18) if split else 1.0
    values = jax.random.normal(key, extent, jnp.float32) * scale * factor_of
    return jnp.minimum(jnp.maximum(values, -most), most).astype(kind)


def setup_inputs(seed: int = 0) -> dict:
    arg_keys = jax.random.split(jax.random.key(seed), 12)
    pair_rep = scatter_about(arg_keys[0], (N, N, C), 1.0, 6.0, ((0, 128),), jnp.float32)
    pair_mask = draw_pair_mask(jax.random.fold_in(arg_keys[11], 71), 0)
    ln_in_gain = jnp.clip(jax.random.uniform(arg_keys[2], (C,), jnp.float32, 0.5, 1.5), 0.5, 1.5)
    ln_in_bias = scatter_about(arg_keys[3], (C,), 0.5, 3.0, (), jnp.float32)
    w_in = scatter_about(arg_keys[4], (C, 4 * H + C), C ** -0.5, 0.5, (), jnp.float32)
    b_in = scatter_about(arg_keys[5], (4 * H + C,), 0.5, 3.0, (), jnp.float32)
    ln_out_gain = jnp.clip(jax.random.uniform(arg_keys[6], (H,), jnp.float32, 0.5, 1.5), 0.5, 1.5)
    ln_out_bias = scatter_about(arg_keys[7], (H,), 0.5, 3.0, (), jnp.float32)
    w_out = scatter_about(arg_keys[8], (H, C), H ** -0.5, 0.5, (), jnp.float32)
    b_out = scatter_about(arg_keys[9], (C,), 0.5, 3.0, (), jnp.float32)
    cotangent = scatter_about(arg_keys[10], (N, N, C), 1.0, 6.0, ((0, 128),), jnp.float32)
    return {"pair_rep": pair_rep, "pair_mask": pair_mask, "ln_in_gain": ln_in_gain, "ln_in_bias": ln_in_bias, "w_in": w_in, "b_in": b_in, "ln_out_gain": ln_out_gain, "ln_out_bias": ln_out_bias, "w_out": w_out, "b_out": b_out, "cotangent": cotangent}


epsilon = 1e-05

def prelude(field, keep_mask, norm_gain, norm_bias, weights, offsets):
    channels = field.shape[-1]
    hidden = (weights.shape[1] - channels) // 4
    center = lax.optimization_barrier(jnp.mean(field, -1, keepdims=True))
    spread = lax.optimization_barrier(jnp.mean((field - center) ** 2, -1, keepdims=True))
    normed = (field - center) * lax.rsqrt(spread + epsilon) * norm_gain + norm_bias
    pieces = jnp.einsum('ikc,cf->fik', normed, weights[:, :4 * hidden], precision=lax.Precision.HIGHEST)
    pieces = pieces + offsets[:4 * hidden, None, None]
    gate = jax.nn.sigmoid(jnp.einsum('ikc,cf->ikf', normed, weights[:, 4 * hidden:], precision=lax.Precision.HIGHEST) + offsets[4 * hidden:])
    keep = keep_mask.astype(field.dtype)[None]
    left = keep * jax.nn.sigmoid(pieces[:hidden]) * pieces[hidden:2 * hidden]
    right = keep * jax.nn.sigmoid(pieces[2 * hidden:3 * hidden]) * pieces[3 * hidden:]
    return (left, right, gate)

def epilogue(product, gate, norm_gain, norm_bias, weights, offset):
    center = lax.optimization_barrier(jnp.mean(product, 0, keepdims=True))
    spread = lax.optimization_barrier(jnp.mean((product - center) ** 2, 0, keepdims=True))
    normed = (product - center) * lax.rsqrt(spread + epsilon) * norm_gain[:, None, None] + norm_bias[:, None, None]
    projected = jnp.einsum('hij,hc->ijc', normed, weights, precision=lax.Precision.HIGHEST) + offset
    return gate * projected

def reference(pair_rep, pair_mask, ln_in_gain, ln_in_bias, w_in, b_in, ln_out_gain, ln_out_bias, w_out, b_out, cotangent):
    count = N_ROW * N_CH
    row_count = N // count
    field_blocks = pair_rep.reshape(count, row_count, N, C)
    mask_blocks = pair_mask.reshape(count, row_count, N)

    def forward_block(inputs):
        return prelude(inputs[0], inputs[1], ln_in_gain, ln_in_bias, w_in, b_in)
    left, right, gate = lax.map(forward_block, (field_blocks, mask_blocks))
    left_full = left.transpose(1, 0, 2, 3).reshape(H, N, N)
    right_full = right.transpose(1, 0, 2, 3).reshape(H, N, N)
    product = jnp.einsum('hik,hjk->hij', left_full, right_full, precision=lax.Precision.HIGHEST)
    product_blocks = product.reshape(H, count, row_count, N).transpose(1, 0, 2, 3)
    cot_blocks = cotangent.reshape(count, row_count, N, C)

    def epilogue_block(inputs):

        def local(prod_part, gate_part, weights):
            return epilogue(prod_part, gate_part, ln_out_gain, ln_out_bias, weights, b_out)
        result, backward = jax.vjp(local, inputs[0], inputs[1], w_out)
        d_prod, d_gate, d_weights = backward(inputs[2])
        return (result, d_prod, d_gate, d_weights)
    update, d_product, d_gate, wout_parts = lax.map(epilogue_block, (product_blocks, gate, cot_blocks))
    d_full = d_product.transpose(1, 0, 2, 3).reshape(H, N, N)
    d_left = jnp.einsum('hij,hjk->hik', d_full, right_full, precision=lax.Precision.HIGHEST)
    d_right = jnp.einsum('hij,hik->hjk', d_full, left_full, precision=lax.Precision.HIGHEST)
    d_left = d_left.reshape(H, count, row_count, N).transpose(1, 0, 2, 3)
    d_right = d_right.reshape(H, count, row_count, N).transpose(1, 0, 2, 3)

    def backward_block(inputs):

        def local(field, weights):
            return prelude(field, inputs[1], ln_in_gain, ln_in_bias, weights, b_in)
        _, backward = jax.vjp(local, inputs[0], w_in)
        return backward((inputs[2], inputs[3], inputs[4]))
    grad_blocks, win_parts = lax.map(backward_block, (field_blocks, mask_blocks, d_left, d_right, d_gate))
    grad_pair = grad_blocks.reshape(N, N, C)
    grad_w_in = lax.optimization_barrier(jnp.sum(win_parts, 0)) / N
    grad_w_out = lax.optimization_barrier(jnp.sum(wout_parts, 0)) / N
    return (update.reshape(N, N, C), grad_pair, grad_w_in, grad_w_out)
```

```python
import jax
import jax.numpy as jnp
from jax import lax
from jax.sharding import PartitionSpec as P

epsilon = 1e-05


def side_by_side(arrays, axis, split_dim, concat_dim, along):
    ends, at = ([], 0)
    for a in arrays[:-1]:
        at += a.shape[along]
        ends.append(at)
    both = jnp.concatenate(arrays, axis=along)
    return tuple(
        jnp.split(
            lax.all_to_all(both, axis, split_axis=split_dim, concat_axis=concat_dim, tiled=True),
            ends,
            axis=along,
        )
    )


def prelude(field, keep_mask, norm_gain, norm_bias, weights, offsets):
    channels = field.shape[-1]
    hidden = (weights.shape[1] - channels) // 4
    center = jnp.mean(field, -1, keepdims=True)
    spread = jnp.mean((field - center) ** 2, -1, keepdims=True)
    normed = (field - center) * lax.rsqrt(spread + epsilon) * norm_gain + norm_bias
    pieces = jnp.einsum(
        "ikc,cf->fik", normed, weights[:, : 4 * hidden], precision=lax.Precision.HIGHEST
    )
    pieces = pieces + offsets[: 4 * hidden, None, None]
    gate = jax.nn.sigmoid(
        jnp.einsum("ikc,cf->ikf", normed, weights[:, 4 * hidden :], precision=lax.Precision.HIGHEST)
        + offsets[4 * hidden :]
    )
    keep = keep_mask.astype(field.dtype)[None]
    left = keep * jax.nn.sigmoid(pieces[:hidden]) * pieces[hidden : 2 * hidden]
    right = keep * jax.nn.sigmoid(pieces[2 * hidden : 3 * hidden]) * pieces[3 * hidden :]
    return (left, right, gate)


def epilogue(product, gate, norm_gain, norm_bias, weights, offset):
    center = jnp.mean(product, 0, keepdims=True)
    spread = jnp.mean((product - center) ** 2, 0, keepdims=True)
    normed = (product - center) * lax.rsqrt(spread + epsilon) * norm_gain[
        :, None, None
    ] + norm_bias[:, None, None]
    projected = jnp.einsum("hij,hc->ijc", normed, weights, precision=lax.Precision.HIGHEST) + offset
    return gate * projected


def on_device(
    pair_rep,
    pair_mask,
    ln_in_gain,
    ln_in_bias,
    w_in,
    b_in,
    ln_out_gain,
    ln_out_bias,
    w_out,
    b_out,
    cotangent,
):
    row_count = pair_rep.shape[0]
    length = pair_rep.shape[1]
    hidden = w_out.shape[0]
    per_device = hidden // (lax.axis_size("row") * lax.axis_size("ch"))

    def local_prelude(field, weights):
        return prelude(field, pair_mask, ln_in_gain, ln_in_bias, weights, b_in)

    (left_rows, right_rows, gate), prelude_back = jax.vjp(local_prelude, pair_rep, w_in)
    row_shape = (hidden, 1, row_count, length)
    left_cols, right_cols = side_by_side(
        (left_rows.reshape(row_shape), right_rows.reshape(row_shape)), ("row", "ch"), 0, 2, 1
    )
    left_cols = left_cols.reshape(per_device, length, length)
    right_cols = right_cols.reshape(per_device, length, length)
    product = jnp.einsum("hik,hjk->hij", left_cols, right_cols, precision=lax.Precision.HIGHEST)
    product_rows = lax.all_to_all(
        product.reshape(per_device, 1, length, length),
        ("row", "ch"),
        split_axis=2,
        concat_axis=0,
        tiled=True,
    )
    product_rows = product_rows.reshape(hidden, row_count, length)

    def local_epilogue(prod_part, gate_part, weights):
        return epilogue(prod_part, gate_part, ln_out_gain, ln_out_bias, weights, b_out)

    update, epilogue_back = jax.vjp(local_epilogue, product_rows, gate, w_out)
    d_product, d_gate, d_wout = epilogue_back(cotangent)
    d_cols = lax.all_to_all(
        d_product.reshape(row_shape), ("row", "ch"), split_axis=0, concat_axis=2, tiled=True
    )
    d_cols = d_cols.reshape(per_device, length, length)
    d_left = jnp.einsum("hij,hjk->hik", d_cols, right_cols, precision=lax.Precision.HIGHEST)
    d_right = jnp.einsum("hij,hik->hjk", d_cols, left_cols, precision=lax.Precision.HIGHEST)
    col_shape = (per_device, 1, length, length)
    d_left, d_right = side_by_side(
        (d_left.reshape(col_shape), d_right.reshape(col_shape)), ("row", "ch"), 2, 0, 1
    )
    d_left = d_left.reshape(hidden, row_count, length)
    d_right = d_right.reshape(hidden, row_count, length)
    grad_pair, d_win = prelude_back((d_left, d_right, d_gate))
    wide = w_in.shape[1]
    terms = jnp.concatenate([d_win, d_wout], axis=1)
    terms = lax.all_to_all(terms, ("row", "ch"), split_axis=0, concat_axis=0, tiled=True)
    mine = jnp.sum(terms, 0, keepdims=True) / length
    whole = lax.all_to_all(
        jnp.broadcast_to(mine, terms.shape),
        ("row", "ch"),
        split_axis=0,
        concat_axis=0,
        tiled=True,
    )
    return (update, grad_pair, whole[:, :wide], whole[:, wide:])


def solution(mesh):
    placed = (
        P(("row", "ch"), None, None),
        P(("row", "ch"), None),
        P(),
        P(),
        P(),
        P(),
        P(),
        P(),
        P(),
        P(),
        P(("row", "ch"), None, None),
    )
    return jax.shard_map(
        on_device,
        mesh=mesh,
        in_specs=placed,
        out_specs=(P(("row", "ch"), None, None), P(("row", "ch"), None, None), P(), P()),
        check_vma=False,
    )
```

```python
import functools

import jax
import jax.numpy as jnp
from jax import lax
from jax.experimental import pallas as pl
from jax.experimental.pallas import tpu as pltpu
from jax.sharding import PartitionSpec as P

epsilon = 1e-05
LANES = 128
AXES = ("row", "ch")
F32 = jnp.float32
NN = (((1,), (0,)), ((), ()))
NT = (((1,), (1,)), ((), ()))
TN = (((0,), (0,)), ((), ()))


def mm(a, b, dims):
    return lax.dot_general(
        a, b, dims, precision=lax.Precision.HIGHEST, preferred_element_type=F32
    )


def every(start, step):
    return pl.ds(start, LANES, stride=step)


def block(b):
    return slice(b * LANES, (b + 1) * LANES)


def column(row):
    return jnp.transpose(jnp.broadcast_to(row, (LANES, LANES)))


def norm_rows(x):
    center = x - jnp.mean(x, -1, keepdims=True)
    scale = lax.rsqrt(jnp.mean(center * center, -1, keepdims=True) + epsilon)
    return center * scale, scale


def norm_cols(x):
    center = x - jnp.mean(x, 0, keepdims=True)
    scale = lax.rsqrt(jnp.mean(center * center, 0, keepdims=True) + epsilon)
    return center * scale, scale


def project(normed, w_ref, b_ref, part):
    return mm(jnp.transpose(w_ref[:, block(part)]), normed, NT) + jnp.tile(
        column(b_ref[pl.ds(part * LANES, LANES)][None]), (1, normed.shape[0] // LANES)
    )


def cell_mask(mask_ref):
    mask = mask_ref[...].astype(F32)
    return jnp.concatenate([mask[0:1], mask[1:2]], axis=1)


def first_kernel(*refs):
    arrays, out_ref, held, sems = refs[:6], refs[6], refs[7:13], refs[13]
    copies = [pltpu.make_async_copy(a, h, sems.at[n]) for n, (a, h) in enumerate(zip(arrays, held))]
    for copy in copies:
        copy.start()
    x_ref, mask_ref, g_ref, b_ref, w_ref, bin_ref = held
    for n in (0, 1, 2, 3, 5, 4):
        copies[n].wait()
    hat, _ = norm_rows(x_ref[...])
    normed = hat * g_ref[...] + b_ref[...]
    mask = cell_mask(mask_ref)
    for side in range(2):
        value = (
            mask
            * jax.nn.sigmoid(project(normed, w_ref, bin_ref, 2 * side))
            * project(normed, w_ref, bin_ref, 2 * side + 1)
        )
        for b in range(4):
            out_ref[every(4 * side + b, 8), :] = value[:, block(b)]


def side_kernel(
    x_ref, mask_ref, g_ref, b_ref, w_ref, bin_ref, cot_ref, wout_ref, gout_ref,
    normed_ref, factor_ref, gate_ref, back_ref, cg_ref,
):
    hat, _ = norm_rows(x_ref[...])
    normed = hat * g_ref[...] + b_ref[...]
    normed_ref[...] = normed
    mask = cell_mask(mask_ref)
    for side in range(2):
        sig = jax.nn.sigmoid(project(normed, w_ref, bin_ref, 2 * side))
        value = project(normed, w_ref, bin_ref, 2 * side + 1)
        open_part = mask * sig
        factor_ref[block(2 * side), :] = open_part * (1.0 - sig) * value
        factor_ref[block(2 * side + 1), :] = open_part
    gate = jax.nn.sigmoid(mm(normed, w_ref[:, block(4)], NN) + bin_ref[pl.ds(4 * LANES, LANES)][None])
    gate_ref[...] = gate
    cg_ref[...] = gate * cot_ref[...]
    gain = column(gout_ref[...])
    for q in range(4):
        part = cg_ref[every((q // 2) * 256 + q % 2, 2), :]
        back_ref[:, block(q)] = gain * mm(wout_ref[...], part, NT)


def gather_sides(in_ref):
    sides = []
    for side in range(2):
        rows = [
            jnp.concatenate([in_ref[every(4 * side + 2 * r + h, 8), :] for h in range(2)], axis=1)
            for r in range(2)
        ]
        sides.append(jnp.concatenate(rows, axis=0))
    return sides


def product_kernel(in_ref, out_ref):
    left, right = gather_sides(in_ref)
    product = mm(left, right, NT)
    for q in range(4):
        out_ref[every(q, 4), :] = product[block(q // 2), block(q % 2)]


def middle_kernel(in_ref, back_ref, out_ref):
    for q in range(4):
        hat, scale = norm_cols(in_ref[every(q, 4), :])
        back = back_ref[:, block(q)]
        first = jnp.mean(back, 0, keepdims=True)
        second = jnp.mean(back * hat, 0, keepdims=True)
        out_ref[every(q, 4), :] = scale * (back - first - hat * second)


def update_kernel(
    in_ref, gate_ref, cot_ref, cg_ref, normed_ref, wout_ref, gout_ref, bout_ref, boff_ref, w_ref,
    update_ref, grads_ref, dnorm_ref,
):
    gain, bias = column(gout_ref[...]), column(boff_ref[...])
    d_wout = jnp.zeros((LANES, LANES), F32)
    d_gate_w = jnp.zeros((LANES, LANES), F32)
    for q in range(4):
        cells = every((q // 2) * 256 + q % 2, 2)
        hat, _ = norm_cols(in_ref[every(q, 4), :])
        normed_product = hat * gain + bias
        projected = mm(normed_product, wout_ref[...], TN) + bout_ref[...]
        gate = gate_ref[cells, :]
        update_ref[cells, :] = gate * projected
        d_wout += mm(normed_product, cg_ref[cells, :], NN)
        d_open = cot_ref[cells, :] * projected * gate * (1.0 - gate)
        d_gate_w += mm(normed_ref[cells, :], d_open, TN)
        dnorm_ref[cells, :] = mm(d_open, w_ref[:, block(4)], NT)
    grads_ref[block(0), :] = d_wout
    grads_ref[block(1), :] = d_gate_w


def back_product_kernel(grad_ref, in_ref, out_ref):
    left, right = gather_sides(in_ref)
    grad = jnp.concatenate(
        [
            jnp.concatenate([grad_ref[every(2 * r + c, 4), :] for c in range(2)], axis=1)
            for r in range(2)
        ],
        axis=0,
    )
    sides = (mm(grad, right, NN), mm(grad, left, TN))
    for side in range(2):
        for b in range(4):
            out_ref[every(4 * side + b, 8), :] = sides[side][block(b // 2), block(b % 2)]


def piece_grads(in_ref, factor_ref):
    parts = []
    for side in range(2):
        grad = jnp.concatenate([in_ref[every(4 * side + b, 8), :] for b in range(4)], axis=1)
        parts += [grad * factor_ref[block(2 * side + m), :] for m in range(2)]
    return jnp.concatenate(parts, axis=0)


def weight_kernel(in_ref, factor_ref, normed_ref, extra_ref, out_ref):
    terms = mm(piece_grads(in_ref, factor_ref), normed_ref[...], NN)
    for part in range(4):
        out_ref[every(part, 6), :] = terms[block(part), :]
    for part in range(2):
        out_ref[every(4 + part, 6), :] = extra_ref[block(part), :]


def pair_kernel(in_ref, factor_ref, dnorm_ref, x_ref, g_ref, w_ref, out_ref):
    grads = piece_grads(in_ref, factor_ref)
    d_normed = jnp.transpose(mm(w_ref[:, : 4 * LANES], grads, NN)) + dnorm_ref[...]
    hat, scale = norm_rows(x_ref[...])
    d_hat = d_normed * g_ref[...]
    first = jnp.mean(d_hat, -1, keepdims=True)
    second = jnp.mean(d_hat * hat, -1, keepdims=True)
    out_ref[...] = scale * (d_hat - first - hat * second)


def sum_kernel(length, in_ref, out_ref):
    terms = in_ref[...]
    total = jnp.sum(terms.reshape(LANES // 4, 24, LANES), 0)
    mine = (total[0:6] + total[6:12]) + (total[12:18] + total[18:24])
    mine = jnp.concatenate([mine] * 4, axis=0) * (1.0 / length)
    out_ref[...] = jnp.broadcast_to(mine[None], (LANES // 4, 24, LANES)).reshape(terms.shape)


def last_kernel(in_ref, win_ref, wout_ref):
    for part in range(4):
        win_ref[:, block(part)] = jnp.transpose(in_ref[every(part, 6), :])
    wout_ref[...] = in_ref[every(4, 6), :]
    win_ref[:, block(4)] = in_ref[every(5, 6), :]


def call(kernel, outs, *args):
    many = isinstance(outs, list)
    shapes = [jax.ShapeDtypeStruct(s, F32) for s in (outs if many else [outs])]
    spec = pl.BlockSpec(memory_space=pltpu.VMEM)
    return pl.pallas_call(
        kernel,
        out_shape=shapes if many else shapes[0],
        in_specs=[spec] * len(args),
        out_specs=[spec] * len(shapes) if many else spec,
        compiler_params=pltpu.CompilerParams(vmem_limit_bytes=24 * 2**20),
    )(*args)


def exchange(x):
    return lax.all_to_all(x, AXES, split_axis=0, concat_axis=0, tiled=True)


def exchange_pairs(x):
    return exchange(x.reshape(-1, 2, LANES)).reshape(x.shape)


def on_device(
    pair_rep,
    pair_mask,
    ln_in_gain,
    ln_in_bias,
    w_in,
    b_in,
    ln_out_gain,
    ln_out_bias,
    w_out,
    b_out,
    cotangent,
):
    length = pair_rep.shape[1]
    cells = pair_rep.shape[0] * length
    x = pair_rep.reshape(cells, LANES)
    cot = cotangent.reshape(cells, LANES)
    g_in, o_in = ln_in_gain[None], ln_in_bias[None]
    g_out, o_out = ln_out_gain[None], ln_out_bias[None]
    bias_out = b_out[None]

    inputs = (x, pair_mask, g_in, o_in, w_in, b_in)
    sent = pl.pallas_call(
        first_kernel,
        out_shape=jax.ShapeDtypeStruct((8 * LANES, LANES), F32),
        in_specs=[pl.BlockSpec(memory_space=pltpu.HBM)] * len(inputs),
        out_specs=pl.BlockSpec(memory_space=pltpu.VMEM),
        scratch_shapes=[pltpu.VMEM(a.shape, a.dtype) for a in inputs]
        + [pltpu.SemaphoreType.DMA((len(inputs),))],
        compiler_params=pltpu.CompilerParams(vmem_limit_bytes=24 * 2**20),
    )(*[pltpu.with_memory_space_constraint(a, pltpu.HBM) for a in inputs])
    sides = exchange(sent)
    normed, factor, gate, back, cg = call(
        side_kernel,
        [(cells, LANES), (4 * LANES, cells), (cells, LANES), (LANES, cells), (cells, LANES)],
        *inputs,
        cot,
        w_out,
        g_out,
    )
    product = exchange(call(product_kernel, (4 * LANES, LANES), sides))
    d_product = exchange(call(middle_kernel, (4 * LANES, LANES), product, back))
    update, extra, d_norm = call(
        update_kernel,
        [(cells, LANES), (2 * LANES, LANES), (cells, LANES)],
        product,
        gate,
        cot,
        cg,
        normed,
        w_out,
        g_out,
        bias_out,
        o_out,
        w_in,
    )
    d_sides = exchange(call(back_product_kernel, (8 * LANES, LANES), d_product, sides))
    terms = exchange_pairs(
        call(weight_kernel, (6 * LANES, LANES), d_sides, factor, normed, extra)
    )
    grad_pair = call(
        pair_kernel, (cells, LANES), d_sides, factor, d_norm, x, g_in, w_in
    )
    whole = exchange_pairs(
        call(functools.partial(sum_kernel, length), (6 * LANES, LANES), terms)
    )
    d_win, d_wout = call(last_kernel, [w_in.shape, w_out.shape], whole)
    return (update.reshape(pair_rep.shape), grad_pair.reshape(pair_rep.shape), d_win, d_wout)


def solution(mesh):
    placed = (
        P(("row", "ch"), None, None),
        P(("row", "ch"), None),
        P(),
        P(),
        P(),
        P(),
        P(),
        P(),
        P(),
        P(),
        P(("row", "ch"), None, None),
    )
    return jax.shard_map(
        on_device,
        mesh=mesh,
        in_specs=placed,
        out_specs=(P(("row", "ch"), None, None), P(("row", "ch"), None, None), P(), P()),
        check_vma=False,
    )
```

```python
import functools

import jax
import jax.numpy as jnp
from jax import lax
from jax.experimental import pallas as pl
from jax.experimental.pallas import tpu as pltpu
from jax.sharding import PartitionSpec as P

epsilon = 1e-05
LANES = 128
PARTS = ("x_high", "z", "y", "x_low", "core")
SIZES = (2, 4, 4, 2, 2)
AXES = ("x_low", "core", "x_high", "y", "z")
F32 = jnp.float32
NN = (((1,), (0,)), ((), ()))
NT = (((1,), (1,)), ((), ()))
TN = (((0,), (0,)), ((), ()))


def mm(a, b, dims):
    return lax.dot_general(
        a, b, dims, precision=lax.Precision.HIGHEST, preferred_element_type=F32
    )


def halves(x):
    high = x.astype(jnp.bfloat16)
    return high, (x - high.astype(F32)).astype(jnp.bfloat16)


def mm3(a, b, dims):
    (a_high, a_low), (b_high, b_low) = halves(a), halves(b)
    ((a_dim,), (b_dim,)), _ = dims
    return lax.dot_general(
        jnp.concatenate([a_high, a_low, a_high], axis=a_dim),
        jnp.concatenate([b_high, b_high, b_low], axis=b_dim),
        dims,
        preferred_element_type=F32,
    )


def every(start, step):
    return pl.ds(start, LANES, stride=step)


def block(b):
    return slice(b * LANES, (b + 1) * LANES)


def column(row):
    return jnp.transpose(jnp.broadcast_to(row, (LANES, LANES)))


def norm_rows(x):
    center = x - jnp.mean(x, -1, keepdims=True)
    scale = lax.rsqrt(jnp.mean(center * center, -1, keepdims=True) + epsilon)
    return center * scale, scale


def norm_cols(x):
    center = x - jnp.mean(x, 0, keepdims=True)
    scale = lax.rsqrt(jnp.mean(center * center, 0, keepdims=True) + epsilon)
    return center * scale, scale


def places():
    s = lax.broadcasted_iota(jnp.int32, (LANES, LANES), 0)
    d = lax.broadcasted_iota(jnp.int32, (LANES, LANES), 1)
    x_low_core, x_high, y, z = s // 32, (s // 16) % 2, (s // 4) % 4, s % 4
    return (d == x_high * 64 + z * 16 + y * 4 + x_low_core).astype(F32)


def project(normed, w_ref, b_ref, part, mul=mm):
    return mul(jnp.transpose(w_ref[:, block(part)]), normed, NT) + jnp.tile(
        column(b_ref[pl.ds(part * LANES, LANES)][None]), (1, normed.shape[0] // LANES)
    )


def cell_mask(mask_ref):
    mask = mask_ref[...].astype(F32)
    return jnp.concatenate([mask[0:1], mask[1:2]], axis=1)


def first_kernel(*refs):
    arrays, out_ref, held, sems = refs[:6], refs[6], refs[7:13], refs[13]
    copies = [pltpu.make_async_copy(a, h, sems.at[n]) for n, (a, h) in enumerate(zip(arrays, held))]
    for copy in copies:
        copy.start()
    x_ref, mask_ref, g_ref, b_ref, w_ref, bin_ref = held
    for n in (0, 1, 2, 3, 5, 4):
        copies[n].wait()
    hat, _ = norm_rows(x_ref[...])
    normed = hat * g_ref[...] + b_ref[...]
    mask = cell_mask(mask_ref)
    for side in range(2):
        value = (
            mask
            * jax.nn.sigmoid(project(normed, w_ref, bin_ref, 2 * side, mm3))
            * project(normed, w_ref, bin_ref, 2 * side + 1, mm3)
        )
        for b in range(4):
            out_ref[every(4 * side + b, 8), :] = value[:, block(b)]


def side_kernel(
    x_ref, g_ref, b_ref, w_ref, bin_ref, cot_ref, wout_ref, gout_ref, back_ref, cg_ref, held_ref,
):
    hat, _ = norm_rows(x_ref[...])
    normed = hat * g_ref[...] + b_ref[...]
    held_ref[...] = cot_ref[...] * gate_of(normed, w_ref, bin_ref)
    gain = column(gout_ref[...])
    place = places()
    for q in range(4):
        part = mm(place, held_ref[every((q // 2) * 256 + q % 2, 2), :], NN)
        cg_ref[block(q), :] = part
        back_ref[:, block(q)] = gain * mm(wout_ref[...], part, NT)


def gate_of(normed, w_ref, bin_ref):
    return jax.nn.sigmoid(
        mm(normed, w_ref[:, block(4)], NN) + bin_ref[pl.ds(4 * LANES, LANES)][None]
    )


def gather_sides(in_ref):
    sides = []
    for side in range(2):
        rows = [
            jnp.concatenate([in_ref[every(4 * side + 2 * r + h, 8), :] for h in range(2)], axis=1)
            for r in range(2)
        ]
        sides.append(jnp.concatenate(rows, axis=0))
    return sides


def product_kernel(in_ref, out_ref):
    left, right = gather_sides(in_ref)
    product = mm3(left, right, NT)
    for q in range(4):
        out_ref[every(q, 4), :] = product[block(q // 2), block(q % 2)]


def middle_kernel(in_ref, back_ref, out_ref):
    for q in range(4):
        hat, scale = norm_cols(in_ref[every(q, 4), :])
        back = back_ref[:, block(q)]
        first = jnp.mean(back, 0, keepdims=True)
        second = jnp.mean(back * hat, 0, keepdims=True)
        out_ref[every(q, 4), :] = scale * (back - first - hat * second)


def update_kernel(
    in_ref, x_ref, mask_ref, g_ref, b_ref, w_ref, bin_ref, cot_ref, cg_ref,
    wout_ref, gout_ref, boff_ref, bout_ref,
    update_ref, dnorm_ref, kept_ref, factor_ref, gate_ref,
):
    hat, _ = norm_rows(x_ref[...])
    normed = hat * g_ref[...] + b_ref[...]
    kept_ref[0 : normed.shape[0], :] = normed
    gate_ref[...] = gate_of(normed, w_ref, bin_ref)
    mask = cell_mask(mask_ref)
    for side in range(2):
        sig = jax.nn.sigmoid(project(normed, w_ref, bin_ref, 2 * side))
        value = project(normed, w_ref, bin_ref, 2 * side + 1)
        open_part = mask * sig
        factor_ref[block(2 * side), :] = open_part * (1.0 - sig) * value
        factor_ref[block(2 * side + 1), :] = open_part
    gain, bias = column(gout_ref[...]), column(boff_ref[...])
    place = places()
    d_wout = jnp.zeros((LANES, LANES), F32)
    d_gate_w = jnp.zeros((LANES, LANES), F32)
    for q in range(4):
        cells = every((q // 2) * 256 + q % 2, 2)
        hat, _ = norm_cols(in_ref[every(q, 4), :])
        normed_product = hat * gain + bias
        d_wout += mm(normed_product, cg_ref[block(q), :], NN)
        projected = mm(place, mm(normed_product, wout_ref[...], TN), TN) + bout_ref[...]
        gate = gate_ref[cells, :]
        update_ref[cells, :] = gate * projected
        d_open = cot_ref[cells, :] * projected * gate * (1.0 - gate)
        d_gate_w += mm(kept_ref[cells, :], d_open, TN)
        dnorm_ref[cells, :] = mm(d_open, w_ref[:, block(4)], NT)
    kept_ref[block(4), :] = d_wout
    kept_ref[block(5), :] = d_gate_w


def back_product_kernel(grad_ref, in_ref, out_ref):
    left, right = gather_sides(in_ref)
    grad = jnp.concatenate(
        [
            jnp.concatenate([grad_ref[every(2 * r + c, 4), :] for c in range(2)], axis=1)
            for r in range(2)
        ],
        axis=0,
    )
    sides = (mm3(grad, right, NN), mm3(jnp.transpose(grad), left, NN))
    for side in range(2):
        for b in range(4):
            out_ref[every(4 * side + b, 8), :] = sides[side][block(b // 2), block(b % 2)]


def piece_grads(in_ref, factor_ref):
    parts = []
    for side in range(2):
        grad = jnp.concatenate([in_ref[every(4 * side + b, 8), :] for b in range(4)], axis=1)
        parts += [grad * factor_ref[block(2 * side + m), :] for m in range(2)]
    return jnp.concatenate(parts, axis=0)


def weight_kernel(in_ref, factor_ref, kept_ref, out_ref):
    terms = mm3(piece_grads(in_ref, factor_ref), kept_ref[0 : 4 * LANES, :], NN)
    for part in range(4):
        out_ref[every(part, 6), :] = terms[block(part), :]
    for part in range(2):
        out_ref[every(4 + part, 6), :] = kept_ref[block(4 + part), :]


def pair_kernel(in_ref, factor_ref, dnorm_ref, x_ref, g_ref, w_ref, out_ref):
    grads = piece_grads(in_ref, factor_ref)
    d_normed = jnp.transpose(mm(w_ref[:, : 4 * LANES], grads, NN)) + dnorm_ref[...]
    hat, scale = norm_rows(x_ref[...])
    d_hat = d_normed * g_ref[...]
    first = jnp.mean(d_hat, -1, keepdims=True)
    second = jnp.mean(d_hat * hat, -1, keepdims=True)
    out_ref[...] = scale * (d_hat - first - hat * second)


def sum_kernel(length, in_ref, out_ref):
    terms = in_ref[...]
    total = jnp.sum(terms.reshape(LANES // 4, 24, LANES), 0)
    mine = (total[0:6] + total[6:12]) + (total[12:18] + total[18:24])
    mine = jnp.concatenate([mine] * 4, axis=0) * (1.0 / length)
    out_ref[...] = jnp.broadcast_to(mine[None], (LANES // 4, 24, LANES)).reshape(terms.shape)


def last_kernel(in_ref, win_ref, wout_ref):
    for part in range(4):
        win_ref[:, block(part)] = jnp.transpose(in_ref[every(part, 6), :])
    wout_ref[...] = in_ref[every(4, 6), :]
    win_ref[:, block(4)] = in_ref[every(5, 6), :]


def call(kernel, outs, *args, scratch=()):
    many = isinstance(outs, list)
    shapes = [jax.ShapeDtypeStruct(s, F32) for s in (outs if many else [outs])]
    spec = pl.BlockSpec(memory_space=pltpu.VMEM)
    return pl.pallas_call(
        kernel,
        out_shape=shapes if many else shapes[0],
        in_specs=[spec] * len(args),
        out_specs=[spec] * len(shapes) if many else spec,
        scratch_shapes=[pltpu.VMEM(s, F32) for s in scratch],
        compiler_params=pltpu.CompilerParams(vmem_limit_bytes=24 * 2**20),
    )(*args)


def exchange(x):
    return lax.all_to_all(x, AXES, split_axis=0, concat_axis=0, tiled=True)


def exchange_pairs(x):
    return exchange(x.reshape(-1, 2, LANES)).reshape(x.shape)


def on_device(
    pair_rep,
    pair_mask,
    ln_in_gain,
    ln_in_bias,
    w_in,
    b_in,
    ln_out_gain,
    ln_out_bias,
    w_out,
    b_out,
    cotangent,
):
    length = pair_rep.shape[1]
    cells = pair_rep.shape[0] * length
    x = pair_rep.reshape(cells, LANES)
    cot = cotangent.reshape(cells, LANES)
    g_in, o_in = ln_in_gain[None], ln_in_bias[None]
    g_out, o_out = ln_out_gain[None], ln_out_bias[None]
    bias_out = b_out[None]

    inputs = (x, pair_mask, g_in, o_in, w_in, b_in)
    sent = pl.pallas_call(
        first_kernel,
        out_shape=jax.ShapeDtypeStruct((8 * LANES, LANES), F32),
        in_specs=[pl.BlockSpec(memory_space=pltpu.HBM)] * len(inputs),
        out_specs=pl.BlockSpec(memory_space=pltpu.VMEM),
        scratch_shapes=[pltpu.VMEM(a.shape, a.dtype) for a in inputs]
        + [pltpu.SemaphoreType.DMA((len(inputs),))],
        compiler_params=pltpu.CompilerParams(vmem_limit_bytes=24 * 2**20),
    )(*[pltpu.with_memory_space_constraint(a, pltpu.HBM) for a in inputs])
    sides = exchange(sent)
    back, cg = call(
        side_kernel,
        [(LANES, cells), (cells, LANES)],
        x,
        g_in,
        o_in,
        w_in,
        b_in,
        cot,
        w_out,
        g_out,
        scratch=[(cells, LANES)],
    )
    product = exchange(call(product_kernel, (4 * LANES, LANES), sides))
    d_product = exchange(call(middle_kernel, (4 * LANES, LANES), product, back))
    d_sides = exchange(call(back_product_kernel, (8 * LANES, LANES), d_product, sides))
    update, d_norm, kept, factor = call(
        update_kernel,
        [
            (cells, LANES),
            (cells, LANES),
            (6 * LANES, LANES),
            (4 * LANES, cells),
        ],
        product,
        *inputs,
        cot,
        cg,
        w_out,
        g_out,
        o_out,
        bias_out,
        scratch=[(cells, LANES)],
    )
    terms = exchange_pairs(
        call(weight_kernel, (6 * LANES, LANES), d_sides, factor, kept)
    )
    grad_pair = call(
        pair_kernel, (cells, LANES), d_sides, factor, d_norm, x, g_in, w_in
    )
    whole = exchange_pairs(
        call(functools.partial(sum_kernel, length), (6 * LANES, LANES), terms)
    )
    d_win, d_wout = call(last_kernel, [w_in.shape, w_out.shape], whole)
    return (update.reshape(pair_rep.shape), grad_pair.reshape(pair_rep.shape), d_win, d_wout)


def solution(mesh):
    whole = P(PARTS, None, None)
    placed = (whole, P(PARTS, None)) + (P(),) * 8 + (whole,)
    return jax.shard_map(
        on_device,
        mesh=jax.sharding.Mesh(mesh.devices.reshape(SIZES), PARTS),
        in_specs=placed,
        out_specs=(whole, whole, P(), P()),
        check_vma=False,
    )
```

```python
import functools

import jax
import jax.numpy as jnp
from jax import lax
from jax.experimental import pallas as pl
from jax.experimental.pallas import tpu as pltpu
from jax.sharding import PartitionSpec as P

epsilon = 1e-05
LANES = 128
PARTS = ("x_high", "z", "y", "x_low", "core")
SIZES = (2, 4, 4, 2, 2)
AXES = ("x_low", "core", "x_high", "z", "y")
PLANE = AXES[:4]
LINE = "y"
MEMBERS = 4
SHARE = LANES // MEMBERS
F32 = jnp.float32
NN = (((1,), (0,)), ((), ()))
NT = (((1,), (1,)), ((), ()))
TN = (((0,), (0,)), ((), ()))


def mm(a, b, dims):
    return lax.dot_general(
        a, b, dims, precision=lax.Precision.HIGHEST, preferred_element_type=F32
    )


def halves(x):
    high = x.astype(jnp.bfloat16)
    return high, (x - high.astype(F32)).astype(jnp.bfloat16)


def mm3(a, b, dims):
    (a_high, a_low), (b_high, b_low) = halves(a), halves(b)
    ((a_dim,), (b_dim,)), _ = dims
    return lax.dot_general(
        jnp.concatenate([a_high, a_low, a_high], axis=a_dim),
        jnp.concatenate([b_high, b_high, b_low], axis=b_dim),
        dims,
        preferred_element_type=F32,
    )


def every(start, step):
    return pl.ds(start, LANES, stride=step)


def block(b):
    return slice(b * LANES, (b + 1) * LANES)


def column(row):
    return jnp.transpose(jnp.broadcast_to(row, (LANES, LANES)))


def norm_rows(x):
    center = x - jnp.mean(x, -1, keepdims=True)
    scale = lax.rsqrt(jnp.mean(center * center, -1, keepdims=True) + epsilon)
    return center * scale, scale


def norm_cols(x):
    center = x - jnp.mean(x, 0, keepdims=True)
    scale = lax.rsqrt(jnp.mean(center * center, 0, keepdims=True) + epsilon)
    return center * scale, scale


def places():
    s = lax.broadcasted_iota(jnp.int32, (LANES, LANES), 0)
    d = lax.broadcasted_iota(jnp.int32, (LANES, LANES), 1)
    x_low_core, x_high, z, y = s // 32, (s // 16) % 2, (s // 4) % 4, s % 4
    return (d == x_high * 64 + z * 16 + y * 4 + x_low_core).astype(F32)


def project(normed, w_ref, b_ref, part, mul=mm):
    return mul(jnp.transpose(w_ref[:, block(part)]), normed, NT) + jnp.tile(
        column(b_ref[pl.ds(part * LANES, LANES)][None]), (1, normed.shape[0] // LANES)
    )


def cell_mask(mask_ref):
    mask = mask_ref[...].astype(F32)
    return jnp.concatenate([mask[0:1], mask[1:2]], axis=1)


def first_kernel(x_ref, mask_ref, g_ref, b_ref, w_ref, bin_ref, out_ref, pack_ref):
    hat, _ = norm_rows(x_ref[...])
    normed = hat * g_ref[...] + b_ref[...]
    mask = cell_mask(mask_ref)
    for side in range(2):
        value = (
            mask
            * jax.nn.sigmoid(project(normed, w_ref, bin_ref, 2 * side, mm3))
            * project(normed, w_ref, bin_ref, 2 * side + 1, mm3)
        )
        for b in range(4):
            out_ref[every(4 * side + b, 8), :] = value[:, block(b)]
    pack_ref[0 : 4 * LANES, :] = x_ref[...]
    pack_ref[4 * LANES : 4 * LANES + 8, :] = jnp.concatenate(
        [mask[:, block(b)] for b in range(4)] + [jnp.zeros((4, LANES), F32)], axis=0
    )


def side_kernel(
    x_ref, g_ref, b_ref, w_ref, bin_ref, cot_ref, wout_ref, gout_ref, back_ref, cg_ref, held_ref,
):
    hat, _ = norm_rows(x_ref[...])
    normed = hat * g_ref[...] + b_ref[...]
    held_ref[...] = cot_ref[...] * gate_of(normed, w_ref, bin_ref)
    cg = mm(places(), in_quarters(held_ref), NN)
    for q in range(4):
        cg_ref[block(q), :] = cg[:, block(q)]
    back_ref[...] = jnp.tile(column(gout_ref[...]), (1, 4)) * mm3(wout_ref[...], cg_ref[...], NT)


def quarter(q):
    return every((q // 2) * 256 + q % 2, 2)


def in_quarters(ref):
    return jnp.concatenate([ref[quarter(q), :] for q in range(4)], axis=1)


def gate_of(normed, w_ref, bin_ref):
    return jax.nn.sigmoid(
        mm3(normed, w_ref[:, block(4)], NN) + bin_ref[pl.ds(4 * LANES, LANES)][None]
    )


def gather_sides(in_ref):
    sides = []
    for side in range(2):
        rows = [
            jnp.concatenate([in_ref[every(4 * side + 2 * r + h, 8), :] for h in range(2)], axis=1)
            for r in range(2)
        ]
        sides.append(jnp.concatenate(rows, axis=0))
    return sides


def product_kernel(in_ref, out_ref):
    left, right = gather_sides(in_ref)
    product = mm3(left, right, NT)
    for q in range(4):
        out_ref[every(q, 4), :] = product[block(q // 2), block(q % 2)]


def middle_kernel(in_ref, back_ref, out_ref):
    for q in range(4):
        hat, scale = norm_cols(in_ref[every(q, 4), :])
        back = back_ref[:, block(q)]
        first = jnp.mean(back, 0, keepdims=True)
        second = jnp.mean(back * hat, 0, keepdims=True)
        out_ref[every(q, 4), :] = scale * (back - first - hat * second)


def update_kernel(
    x_ref, g_ref, b_ref, w_ref, bin_ref, cot_ref, wout_ref, gout_ref, boff_ref, bout_ref,
    in_ref, cg_ref,
    update_ref, dnorm_ref, *rest,
):
    extra_refs, (open_ref, gate_ref, grads_ref, held_ref) = rest[:MEMBERS], rest[MEMBERS:]
    hat, _ = norm_rows(x_ref[...])
    normed = hat * g_ref[...] + b_ref[...]
    gate_ref[...] = gate_of(normed, w_ref, bin_ref)
    gain, bias = column(gout_ref[...]), column(boff_ref[...])
    normed_product = jnp.concatenate(
        [norm_cols(in_ref[every(q, 4), :])[0] * gain + bias for q in range(4)], axis=1
    )
    grads_ref[block(0), :] = mm3(normed_product, cg_ref[...], NN)
    projected = mm3(jnp.transpose(normed_product), wout_ref[...], NN)
    projected = jnp.concatenate([projected[block(q), :] for q in range(4)], axis=1)
    projected = mm(places(), projected, TN)
    for q in range(4):
        open_ref[quarter(q), :] = projected[:, block(q)] + bout_ref[...]
    gate = gate_ref[...]
    projected = open_ref[...]
    update_ref[...] = gate * projected
    d_open = cot_ref[...] * projected * gate * (1.0 - gate)
    grads_ref[block(1), :] = mm3(jnp.transpose(normed), d_open, NN)
    dnorm_ref[...] = mm3(d_open, w_ref[:, block(4)], NT)
    for member in range(MEMBERS):
        for part in range(2):
            held_ref[share(2 * member + part), :] = grads_ref[
                pl.ds(part * LANES + member, SHARE, stride=MEMBERS), :
            ]
    for turn in range(MEMBERS):
        extra_refs[turn][...] = held_ref[pl.ds(member_at(turn) * 2 * SHARE, 2 * SHARE), :]


def member_at(turn):
    return lax.rem(lax.axis_index(LINE) + turn, MEMBERS)


def share(n):
    return slice(n * SHARE, (n + 1) * SHARE)


def mine():
    u = lax.broadcasted_iota(jnp.int32, (SHARE, LANES), 0)
    f = lax.broadcasted_iota(jnp.int32, (SHARE, LANES), 1)
    return (f == u * MEMBERS + lax.axis_index(LINE)).astype(F32)


def my_weights(pick, w_ref):
    return jnp.concatenate([mm(pick, w_ref[:, block(p)], NT) for p in range(4)], axis=0)


def factor_kernel(*refs):
    packs, refs = refs[:MEMBERS], refs[MEMBERS:]
    g_ref, b_ref, w_ref, bin_ref, high_ref, low_ref, factor_ref, weights_ref, bias_ref = refs
    pick = mine()
    weights_ref[...] = my_weights(pick, w_ref)
    for p in range(4):
        row = bin_ref[pl.ds(p * LANES, LANES)][None]
        bias_ref[share(p), :] = jnp.broadcast_to(
            jnp.sum(pick * row, axis=1, keepdims=True), (SHARE, LANES)
        )
    for turn in range(MEMBERS):
        pack = packs[turn]
        hat, _ = norm_rows(pack[0 : 4 * LANES, :])
        normed = hat * g_ref[...] + b_ref[...]
        member = member_at(turn)
        rows = pl.ds(pl.multiple_of(member * 4 * LANES, 4 * LANES), 4 * LANES)
        high_ref[rows, :], low_ref[rows, :] = halves(normed)
        pieces = mm3(weights_ref[...], normed, NT) + jnp.tile(bias_ref[...], (1, 4))
        mask = jnp.concatenate([pack[4 * LANES + b : 4 * LANES + b + 1, :] for b in range(4)], axis=1)
        parts = []
        for side in range(2):
            sig = jax.nn.sigmoid(pieces[share(2 * side)])
            open_part = mask * sig
            parts += [open_part * (1.0 - sig) * pieces[share(2 * side + 1)], open_part]
        factor_ref[pl.ds(member * LANES, LANES), :] = jnp.concatenate(parts, axis=0)


def back_product_kernel(grad_ref, in_ref, out_ref):
    left, right = gather_sides(in_ref)
    grad = jnp.concatenate(
        [
            jnp.concatenate([grad_ref[every(2 * r + c, 4), :] for c in range(2)], axis=1)
            for r in range(2)
        ],
        axis=0,
    )
    sides = (mm3(grad, right, NN), mm3(jnp.transpose(grad), left, NN))
    for side in range(2):
        for b in range(4):
            out_ref[every(4 * side + b, 8), :] = sides[side][block(b // 2), block(b % 2)]


def piece_grads(in_ref, factor_ref, member):
    parts = []
    for side in range(2):
        grad = jnp.concatenate(
            [
                in_ref[pl.ds(member * 8 + 4 * side + b, SHARE, stride=8 * MEMBERS), :]
                for b in range(4)
            ],
            axis=1,
        )
        parts += [grad * factor_ref[share(4 * member + 2 * side + m), :] for m in range(2)]
    return jnp.concatenate(parts, axis=0)


def weight_kernel(in_ref, factor_ref, high_ref, low_ref, *refs):
    extras, out_ref = refs[:MEMBERS], refs[MEMBERS]
    grads = jnp.concatenate([piece_grads(in_ref, factor_ref, m) for m in range(MEMBERS)], axis=1)
    high, low = halves(grads)
    terms = sum(
        lax.dot_general(a, b[...], NN, preferred_element_type=F32)
        for a, b in ((high, high_ref), (low, high_ref), (high, low_ref))
    )
    extra = (extras[0][...] + extras[1][...]) + (extras[2][...] + extras[3][...])
    for part in range(4):
        out_ref[pl.ds(part, SHARE, stride=6), :] = terms[share(part), :]
    for part in range(2):
        out_ref[pl.ds(4 + part, SHARE, stride=6), :] = extra[share(part), :]


def cut_kernel(in_ref, *outs):
    for turn in range(MEMBERS):
        first = pl.multiple_of(member_at(turn) * 8, 8)
        rows = in_ref[:, pl.ds(first, 8), :]
        outs[turn][...] = rows.reshape(outs[turn].shape)


def own_kernel(x_ref, mask_ref, g_ref, b_ref, w_ref, bin_ref, hat_ref, scale_ref, factor_ref):
    hat, scale = norm_rows(x_ref[...])
    hat_ref[...] = hat
    scale_ref[...] = jnp.broadcast_to(scale, hat.shape)
    normed = hat * g_ref[...] + b_ref[...]
    mask = cell_mask(mask_ref)
    for side in range(2):
        sig = jax.nn.sigmoid(project(normed, w_ref, bin_ref, 2 * side, mm3))
        value = project(normed, w_ref, bin_ref, 2 * side + 1, mm3)
        open_part = mask * sig
        factor_ref[block(2 * side), :] = open_part * (1.0 - sig) * value
        factor_ref[block(2 * side + 1), :] = open_part


def pair_kernel(
    g_ref, w_ref, dnorm_ref, hat_ref, scale_ref, factor_ref, *refs
):
    cuts, (out_ref, held_ref, sides_ref) = refs[:MEMBERS], refs[MEMBERS:]
    size = 8 * SHARE
    for turn in range(MEMBERS):
        held_ref[pl.ds(member_at(MEMBERS - turn) * size, size), :] = cuts[turn][...]
    for member in range(MEMBERS):
        for n in range(8):
            sides_ref[pl.ds(n * LANES + member, SHARE, stride=MEMBERS), :] = held_ref[
                pl.ds(member * size + n, SHARE, stride=8), :
            ]
    parts = []
    for side in range(2):
        grad = jnp.concatenate([sides_ref[block(4 * side + b), :] for b in range(4)], axis=1)
        parts += [grad * factor_ref[block(2 * side + m), :] for m in range(2)]
    d_normed = mm3(w_ref[:, : 4 * LANES], jnp.concatenate(parts, axis=0), NN)
    d_normed = jnp.transpose(d_normed) + dnorm_ref[...]
    hat = hat_ref[...]
    d_hat = d_normed * g_ref[...]
    first = jnp.mean(d_hat, -1, keepdims=True)
    second = jnp.mean(d_hat * hat, -1, keepdims=True)
    out_ref[...] = scale_ref[...] * (d_hat - first - hat * second)


def sum_kernel(length, in_ref, out_ref):
    terms = in_ref[...]
    total = jnp.sum(terms.reshape(SHARE // 4, 24, LANES), 0)
    mine = (total[0:6] + total[6:12]) + (total[12:18] + total[18:24])
    mine = jnp.concatenate([mine] * 4, axis=0) * (1.0 / length)
    out_ref[...] = jnp.broadcast_to(mine[None], (LANES // 4, 24, LANES)).reshape(out_ref.shape)


def last_kernel(in_ref, win_ref, wout_ref):
    for part in range(4):
        win_ref[:, block(part)] = jnp.transpose(in_ref[every(part, 6), :])
    wout_ref[...] = in_ref[every(4, 6), :]
    win_ref[:, block(4)] = in_ref[every(5, 6), :]


def call(kernel, outs, *args, scratch=(), far=0, work=0):
    many = isinstance(outs, list)
    shapes = [
        jax.ShapeDtypeStruct(s, F32) if isinstance(s, tuple) else s
        for s in (outs if many else [outs])
    ]
    near = pl.BlockSpec(memory_space=pltpu.VMEM)
    held = [pltpu.VMEM(a.shape, a.dtype) for a in args[:far]]

    def body(*refs):
        end = len(args) + len(shapes)
        places = refs[end : end + far]
        copies = [
            pltpu.make_async_copy(refs[n], places[n], refs[-1].at[n]) for n in range(far)
        ]
        for copy in copies:
            copy.start()
        for copy in copies:
            copy.wait()
        kernel(*places, *refs[far:end], *refs[end + far : len(refs) - 1])

    return pl.pallas_call(
        body if far else kernel,
        out_shape=shapes if many else shapes[0],
        in_specs=[pl.BlockSpec(memory_space=pltpu.HBM)] * far + [near] * (len(args) - far),
        out_specs=[near] * len(shapes) if many else near,
        scratch_shapes=held
        + [pltpu.VMEM(s, F32) for s in scratch]
        + ([pltpu.SemaphoreType.DMA((far,))] if far else []),
        cost_estimate=pl.CostEstimate(flops=1000 * work, transcendentals=0, bytes_accessed=work)
        if work
        else None,
        compiler_params=pltpu.CompilerParams(vmem_limit_bytes=24 * 2**20),
    )(*[pltpu.with_memory_space_constraint(a, pltpu.HBM) for a in args[:far]], *args[far:])


def exchange(x, axes=AXES):
    return lax.all_to_all(x, axes, split_axis=0, concat_axis=0, tiled=True)


def exchange_pairs(x, axes=AXES):
    return exchange(x.reshape(-1, 2, LANES), axes).reshape(x.shape)


def fetch(x, turn):
    return lax.ppermute(x, LINE, [((n + turn) % MEMBERS, n) for n in range(MEMBERS)])


def hand(x, turn):
    return lax.ppermute(x, LINE, [(n, (n + turn) % MEMBERS) for n in range(MEMBERS)])


def on_device(
    pair_rep,
    pair_mask,
    ln_in_gain,
    ln_in_bias,
    w_in,
    b_in,
    ln_out_gain,
    ln_out_bias,
    w_out,
    b_out,
    cotangent,
):
    length = pair_rep.shape[1]
    cells = pair_rep.shape[0] * length
    x = pair_rep.reshape(cells, LANES)
    cot = cotangent.reshape(cells, LANES)
    g_in, o_in = ln_in_gain[None], ln_in_bias[None]
    g_out, o_out = ln_out_gain[None], ln_out_bias[None]
    bias_out = b_out[None]

    inputs = (x, pair_mask, g_in, o_in, w_in, b_in)
    sent, pack = call(
        first_kernel, [(8 * LANES, LANES), (cells + 8, LANES)], *inputs, far=len(inputs)
    )
    sides = exchange(sent)
    sides, x_late, pack = lax.optimization_barrier((sides, x, pack))
    back, cg = call(
        side_kernel,
        [(LANES, cells), (cells, LANES)],
        x_late,
        *inputs[2:],
        cot,
        w_out,
        g_out,
        scratch=[(cells, LANES)],
        far=8,
    )
    product = exchange(call(product_kernel, (4 * LANES, LANES), sides))
    packs = [pack] + [fetch(pack, turn) for turn in range(1, MEMBERS)]
    d_product = exchange(call(middle_kernel, (4 * LANES, LANES), product, back))
    update, d_norm, *extras = call(
        update_kernel,
        [(cells, LANES), (cells, LANES)] + [(2 * SHARE, LANES)] * MEMBERS,
        x,
        *inputs[2:],
        cot,
        w_out,
        g_out,
        o_out,
        bias_out,
        product,
        cg,
        far=10,
        scratch=[(cells, LANES), (cells, LANES), (2 * LANES, LANES), (2 * LANES, LANES)],
    )
    high, low, factor = call(
        factor_kernel,
        [jax.ShapeDtypeStruct((MEMBERS * cells, LANES), jnp.bfloat16)] * 2
        + [(MEMBERS * LANES, cells)],
        *packs,
        g_in,
        o_in,
        w_in,
        b_in,
        scratch=[(LANES, LANES), (LANES, LANES)],
        far=8,
    )
    d_product, high, low, factor, extras = lax.optimization_barrier(
        (d_product, high, low, factor, extras)
    )
    extras = [extras[0]] + [hand(extras[turn], turn) for turn in range(1, MEMBERS)]
    d_sides = exchange(call(back_product_kernel, (8 * LANES, LANES), d_product, sides), PLANE)
    terms = call(weight_kernel, (6 * SHARE, LANES), d_sides, factor, high, low, *extras)
    terms, d_sides = lax.optimization_barrier((terms, d_sides))
    terms = exchange_pairs(terms, PLANE)
    cuts = call(
        cut_kernel,
        [(8 * SHARE, LANES)] * MEMBERS,
        d_sides.reshape(SHARE, 8 * MEMBERS, LANES),
    )
    terms, inputs = lax.optimization_barrier((terms, inputs))
    own = call(
        own_kernel, [(cells, LANES), (cells, LANES), (4 * LANES, cells)], *inputs, far=6, work=10**7,
    )
    cuts = [cuts[0]] + [hand(cuts[turn], turn) for turn in range(1, MEMBERS)]
    grad_pair = call(
        pair_kernel,
        (cells, LANES),
        g_in,
        w_in,
        d_norm,
        *own,
        *cuts,
        scratch=[(8 * LANES, LANES), (8 * LANES, LANES)],
        far=3,
    )
    whole = exchange_pairs(
        call(functools.partial(sum_kernel, length), (6 * LANES, LANES), terms)
    )
    d_win, d_wout = call(last_kernel, [w_in.shape, w_out.shape], whole)
    return (update.reshape(pair_rep.shape), grad_pair.reshape(pair_rep.shape), d_win, d_wout)


def solution(mesh):
    whole = P(PARTS, None, None)
    placed = (whole, P(PARTS, None)) + (P(),) * 8 + (whole,)
    return jax.shard_map(
        on_device,
        mesh=jax.sharding.Mesh(mesh.devices.reshape(SIZES), PARTS),
        in_specs=placed,
        out_specs=(whole, whole, P(), P()),
        check_vma=False,
    )
```

```python
import functools

import jax
import jax.numpy as jnp
from jax import lax
from jax.experimental import pallas as pl
from jax.experimental.pallas import tpu as pltpu
from jax.sharding import PartitionSpec as P

epsilon = 1e-05
LANES = 128
PARTS = ("x_high", "z", "y", "x_low", "core")
SIZES = (2, 4, 4, 2, 2)
AXES = ("x_low", "core", "x_high", "z", "y")
PLANE = AXES[:4]
LINE = "y"
MEMBERS = 4
SHARE = LANES // MEMBERS
F32 = jnp.float32
NN = (((1,), (0,)), ((), ()))
NT = (((1,), (1,)), ((), ()))
TN = (((0,), (0,)), ((), ()))


def mm(a, b, dims):
    return lax.dot_general(
        a, b, dims, precision=lax.Precision.HIGHEST, preferred_element_type=F32
    )


def halves(x):
    high = x.astype(jnp.bfloat16)
    return high, (x - high.astype(F32)).astype(jnp.bfloat16)


def mm3(a, b, dims):
    (a_high, a_low), (b_high, b_low) = halves(a), halves(b)
    ((a_dim,), (b_dim,)), _ = dims
    return lax.dot_general(
        jnp.concatenate([a_high, a_low, a_high], axis=a_dim),
        jnp.concatenate([b_high, b_high, b_low], axis=b_dim),
        dims,
        preferred_element_type=F32,
    )


def every(start, step):
    return pl.ds(start, LANES, stride=step)


def block(b):
    return slice(b * LANES, (b + 1) * LANES)


def column(row):
    return jnp.transpose(jnp.broadcast_to(row, (LANES, LANES)))


def norm_rows(x):
    center = x - jnp.mean(x, -1, keepdims=True)
    scale = lax.rsqrt(jnp.mean(center * center, -1, keepdims=True) + epsilon)
    return center * scale, scale


def norm_cols(x):
    center = x - jnp.mean(x, 0, keepdims=True)
    scale = lax.rsqrt(jnp.mean(center * center, 0, keepdims=True) + epsilon)
    return center * scale, scale


def places():
    s = lax.broadcasted_iota(jnp.int32, (LANES, LANES), 0)
    d = lax.broadcasted_iota(jnp.int32, (LANES, LANES), 1)
    x_low_core, x_high, z, y = s // 32, (s // 16) % 2, (s // 4) % 4, s % 4
    return (d == x_high * 64 + z * 16 + y * 4 + x_low_core).astype(F32)


def project(normed, w_ref, b_ref, part, mul=mm):
    return mul(jnp.transpose(w_ref[:, block(part)]), normed, NT) + jnp.tile(
        column(b_ref[pl.ds(part * LANES, LANES)][None]), (1, normed.shape[0] // LANES)
    )


def cell_mask(mask_ref):
    mask = mask_ref[...].astype(F32)
    return jnp.concatenate([mask[0:1], mask[1:2]], axis=1)


def first_kernel(x_ref, mask_ref, g_ref, b_ref, w_ref, bin_ref, out_ref, pack_ref):
    hat, _ = norm_rows(x_ref[...])
    normed = hat * g_ref[...] + b_ref[...]
    mask = cell_mask(mask_ref)
    weights = jnp.concatenate([jnp.transpose(w_ref[:, block(p)]) for p in range(4)], axis=0)
    bias = jnp.concatenate(
        [column(bin_ref[pl.ds(p * LANES, LANES)][None]) for p in range(4)], axis=0
    )
    pieces = mm3(weights, normed, NT) + jnp.tile(bias, (1, 4))
    for side in range(2):
        value = mask * jax.nn.sigmoid(pieces[block(2 * side)]) * pieces[block(2 * side + 1)]
        for b in range(4):
            out_ref[every(4 * side + b, 8), :] = value[:, block(b)]
    pack_ref[0 : 4 * LANES, :] = x_ref[...]
    pack_ref[4 * LANES : 4 * LANES + 8, :] = jnp.concatenate(
        [mask[:, block(b)] for b in range(4)] + [jnp.zeros((4, LANES), F32)], axis=0
    )


def side_kernel(
    x_ref, g_ref, b_ref, w_ref, bin_ref, cot_ref, wout_ref, gout_ref, back_ref, cg_ref, held_ref,
):
    hat, _ = norm_rows(x_ref[...])
    normed = hat * g_ref[...] + b_ref[...]
    held_ref[...] = cot_ref[...] * gate_of(normed, w_ref, bin_ref)
    cg = mm(places(), in_quarters(held_ref), NN)
    for q in range(4):
        cg_ref[block(q), :] = cg[:, block(q)]
    back_ref[...] = jnp.tile(column(gout_ref[...]), (1, 4)) * mm3(wout_ref[...], cg_ref[...], NT)


def quarter(q):
    return every((q // 2) * 256 + q % 2, 2)


def in_quarters(ref):
    return jnp.concatenate([ref[quarter(q), :] for q in range(4)], axis=1)


def gate_of(normed, w_ref, bin_ref):
    return jax.nn.sigmoid(
        mm3(normed, w_ref[:, block(4)], NN) + bin_ref[pl.ds(4 * LANES, LANES)][None]
    )


def gather_sides(in_ref):
    sides = []
    for side in range(2):
        rows = [
            jnp.concatenate([in_ref[every(4 * side + 2 * r + h, 8), :] for h in range(2)], axis=1)
            for r in range(2)
        ]
        sides.append(jnp.concatenate(rows, axis=0))
    return sides


def product_kernel(in_ref, out_ref):
    left, right = gather_sides(in_ref)
    product = mm3(left, right, NT)
    for q in range(4):
        out_ref[every(q, 4), :] = product[block(q // 2), block(q % 2)]


def middle_kernel(in_ref, back_ref, out_ref):
    for q in range(4):
        hat, scale = norm_cols(in_ref[every(q, 4), :])
        back = back_ref[:, block(q)]
        first = jnp.mean(back, 0, keepdims=True)
        second = jnp.mean(back * hat, 0, keepdims=True)
        out_ref[every(q, 4), :] = scale * (back - first - hat * second)


def update_kernel(
    x_ref, g_ref, b_ref, w_ref, bin_ref, cot_ref, wout_ref, gout_ref, boff_ref, bout_ref,
    in_ref, cg_ref,
    update_ref, dnorm_ref, *rest,
):
    extra_refs, (open_ref, gate_ref, grads_ref, held_ref) = rest[:MEMBERS], rest[MEMBERS:]
    hat, _ = norm_rows(x_ref[...])
    normed = hat * g_ref[...] + b_ref[...]
    gate_ref[...] = gate_of(normed, w_ref, bin_ref)
    gain, bias = column(gout_ref[...]), column(boff_ref[...])
    normed_product = jnp.concatenate(
        [norm_cols(in_ref[every(q, 4), :])[0] * gain + bias for q in range(4)], axis=1
    )
    grads_ref[block(0), :] = mm3(normed_product, cg_ref[...], NN)
    projected = mm3(jnp.transpose(normed_product), wout_ref[...], NN)
    projected = jnp.concatenate([projected[block(q), :] for q in range(4)], axis=1)
    projected = mm(places(), projected, TN)
    for q in range(4):
        open_ref[quarter(q), :] = projected[:, block(q)] + bout_ref[...]
    gate = gate_ref[...]
    projected = open_ref[...]
    update_ref[...] = gate * projected
    d_open = cot_ref[...] * projected * gate * (1.0 - gate)
    grads_ref[block(1), :] = mm3(jnp.transpose(normed), d_open, NN)
    dnorm_ref[...] = mm3(d_open, w_ref[:, block(4)], NT)
    for member in range(MEMBERS):
        for part in range(2):
            held_ref[share(2 * member + part), :] = grads_ref[
                pl.ds(part * LANES + member, SHARE, stride=MEMBERS), :
            ]
    for turn in range(MEMBERS):
        extra_refs[turn][...] = held_ref[pl.ds(member_at(turn) * 2 * SHARE, 2 * SHARE), :]


def member_at(turn):
    return lax.rem(lax.axis_index(LINE) + turn, MEMBERS)


def share(n):
    return slice(n * SHARE, (n + 1) * SHARE)


def mine():
    u = lax.broadcasted_iota(jnp.int32, (SHARE, LANES), 0)
    f = lax.broadcasted_iota(jnp.int32, (SHARE, LANES), 1)
    return (f == u * MEMBERS + lax.axis_index(LINE)).astype(F32)


def my_weights(pick, w_ref):
    return jnp.concatenate([mm(pick, w_ref[:, block(p)], NT) for p in range(4)], axis=0)


def factor_kernel(turns, g_ref, b_ref, w_ref, bin_ref, *refs):
    packs, (high_ref, low_ref, factor_ref, weights_ref, bias_ref) = refs[: len(turns)], refs[-5:]
    pick = mine()
    weights_ref[...] = my_weights(pick, w_ref)
    for p in range(4):
        row = bin_ref[pl.ds(p * LANES, LANES)][None]
        bias_ref[share(p), :] = jnp.broadcast_to(
            jnp.sum(pick * row, axis=1, keepdims=True), (SHARE, LANES)
        )
    for pack, turn in zip(packs, turns):
        hat, _ = norm_rows(pack[0 : 4 * LANES, :])
        normed = hat * g_ref[...] + b_ref[...]
        member = member_at(turn)
        rows = pl.ds(pl.multiple_of(member * 4 * LANES, 4 * LANES), 4 * LANES)
        high_ref[rows, :], low_ref[rows, :] = halves(normed)
        pieces = mm3(weights_ref[...], normed, NT) + jnp.tile(bias_ref[...], (1, 4))
        mask = jnp.concatenate([pack[4 * LANES + b : 4 * LANES + b + 1, :] for b in range(4)], axis=1)
        parts = []
        for side in range(2):
            sig = jax.nn.sigmoid(pieces[share(2 * side)])
            open_part = mask * sig
            parts += [open_part * (1.0 - sig) * pieces[share(2 * side + 1)], open_part]
        factor_ref[pl.ds(member * LANES, LANES), :] = jnp.concatenate(parts, axis=0)


def back_product_kernel(grad_ref, in_ref, out_ref):
    left, right = gather_sides(in_ref)
    grad = jnp.concatenate(
        [
            jnp.concatenate([grad_ref[every(2 * r + c, 4), :] for c in range(2)], axis=1)
            for r in range(2)
        ],
        axis=0,
    )
    sides = (mm3(grad, right, NN), mm3(jnp.transpose(grad), left, NN))
    for side in range(2):
        for b in range(4):
            out_ref[every(4 * side + b, 8), :] = sides[side][block(b // 2), block(b % 2)]


def piece_grads(in_ref, factor_ref, member):
    parts = []
    for side in range(2):
        grad = jnp.concatenate(
            [
                in_ref[pl.ds(member * 8 + 4 * side + b, SHARE, stride=8 * MEMBERS), :]
                for b in range(4)
            ],
            axis=1,
        )
        parts += [grad * factor_ref[share(4 * member + 2 * side + m), :] for m in range(2)]
    return jnp.concatenate(parts, axis=0)


def weight_kernel(in_ref, factor_ref, high_ref, low_ref, *refs):
    extras, out_ref = refs[:MEMBERS], refs[MEMBERS]
    grads = jnp.concatenate([piece_grads(in_ref, factor_ref, m) for m in range(MEMBERS)], axis=1)
    high, low = halves(grads)
    terms = sum(
        lax.dot_general(a, b[...], NN, preferred_element_type=F32)
        for a, b in ((high, high_ref), (low, high_ref), (high, low_ref))
    )
    extra = (extras[0][...] + extras[1][...]) + (extras[2][...] + extras[3][...])
    for part in range(4):
        out_ref[pl.ds(part, SHARE, stride=6), :] = terms[share(part), :]
    for part in range(2):
        out_ref[pl.ds(4 + part, SHARE, stride=6), :] = extra[share(part), :]


def cut_kernel(in_ref, *outs):
    for turn in range(MEMBERS):
        first = pl.multiple_of(member_at(turn) * 8, 8)
        rows = in_ref[:, pl.ds(first, 8), :]
        outs[turn][...] = rows.reshape(outs[turn].shape)


def own_kernel(x_ref, mask_ref, g_ref, b_ref, w_ref, bin_ref, hat_ref, scale_ref, factor_ref):
    hat, scale = norm_rows(x_ref[...])
    hat_ref[...] = hat
    scale_ref[...] = jnp.broadcast_to(scale, hat.shape)
    normed = hat * g_ref[...] + b_ref[...]
    mask = cell_mask(mask_ref)
    for side in range(2):
        sig = jax.nn.sigmoid(project(normed, w_ref, bin_ref, 2 * side, mm3))
        value = project(normed, w_ref, bin_ref, 2 * side + 1, mm3)
        open_part = mask * sig
        factor_ref[block(2 * side), :] = open_part * (1.0 - sig) * value
        factor_ref[block(2 * side + 1), :] = open_part


def pair_kernel(
    g_ref, w_ref, dnorm_ref, hat_ref, scale_ref, factor_ref, *refs
):
    cuts, (out_ref, held_ref, sides_ref) = refs[:MEMBERS], refs[MEMBERS:]
    size = 8 * SHARE
    for turn in range(MEMBERS):
        held_ref[pl.ds(member_at(MEMBERS - turn) * size, size), :] = cuts[turn][...]
    for member in range(MEMBERS):
        for n in range(8):
            sides_ref[pl.ds(n * LANES + member, SHARE, stride=MEMBERS), :] = held_ref[
                pl.ds(member * size + n, SHARE, stride=8), :
            ]
    parts = []
    for side in range(2):
        grad = jnp.concatenate([sides_ref[block(4 * side + b), :] for b in range(4)], axis=1)
        parts += [grad * factor_ref[block(2 * side + m), :] for m in range(2)]
    d_normed = mm3(w_ref[:, : 4 * LANES], jnp.concatenate(parts, axis=0), NN)
    d_normed = jnp.transpose(d_normed) + dnorm_ref[...]
    hat = hat_ref[...]
    d_hat = d_normed * g_ref[...]
    first = jnp.mean(d_hat, -1, keepdims=True)
    second = jnp.mean(d_hat * hat, -1, keepdims=True)
    out_ref[...] = scale_ref[...] * (d_hat - first - hat * second)


def sum_kernel(length, in_ref, out_ref):
    terms = in_ref[...]
    total = jnp.sum(terms.reshape(SHARE // 4, 24, LANES), 0)
    mine = (total[0:6] + total[6:12]) + (total[12:18] + total[18:24])
    mine = jnp.concatenate([mine] * 4, axis=0) * (1.0 / length)
    out_ref[...] = jnp.broadcast_to(mine[None], (LANES // 4, 24, LANES)).reshape(out_ref.shape)


def last_kernel(in_ref, win_ref, wout_ref):
    for part in range(4):
        win_ref[:, block(part)] = jnp.transpose(in_ref[every(part, 6), :])
    wout_ref[...] = in_ref[every(4, 6), :]
    win_ref[:, block(4)] = in_ref[every(5, 6), :]


def call(kernel, outs, *given, args=(), scratch=(), far=0, work=0, aliases={}):
    args = (*given, *args)
    many = isinstance(outs, list)
    shapes = [
        jax.ShapeDtypeStruct(s, F32) if isinstance(s, tuple) else s
        for s in (outs if many else [outs])
    ]
    near = pl.BlockSpec(memory_space=pltpu.VMEM)
    held = [pltpu.VMEM(a.shape, a.dtype) for a in args[:far]]

    def body(*refs):
        end = len(args) + len(shapes)
        places = refs[end : end + far]
        copies = [
            pltpu.make_async_copy(refs[n], places[n], refs[-1].at[n]) for n in range(far)
        ]
        for copy in copies:
            copy.start()
        for copy in copies:
            copy.wait()
        kernel(*places, *refs[far:end], *refs[end + far : len(refs) - 1])

    return pl.pallas_call(
        body if far else kernel,
        out_shape=shapes if many else shapes[0],
        in_specs=[pl.BlockSpec(memory_space=pltpu.HBM)] * far + [near] * (len(args) - far),
        out_specs=[near] * len(shapes) if many else near,
        scratch_shapes=held
        + [pltpu.VMEM(s, F32) for s in scratch]
        + ([pltpu.SemaphoreType.DMA((far,))] if far else []),
        input_output_aliases=aliases,
        cost_estimate=pl.CostEstimate(flops=1000 * work, transcendentals=0, bytes_accessed=work)
        if work
        else None,
        compiler_params=pltpu.CompilerParams(vmem_limit_bytes=24 * 2**20),
    )(*[pltpu.with_memory_space_constraint(a, pltpu.HBM) for a in args[:far]], *args[far:])


def exchange(x, axes=AXES):
    return lax.all_to_all(x, axes, split_axis=0, concat_axis=0, tiled=True)


def exchange_pairs(x, axes=AXES):
    return exchange(x.reshape(-1, 2, LANES), axes).reshape(x.shape)


def fetch(x, turn):
    return lax.ppermute(x, LINE, [((n + turn) % MEMBERS, n) for n in range(MEMBERS)])


def hand(x, turn):
    return lax.ppermute(x, LINE, [(n, (n + turn) % MEMBERS) for n in range(MEMBERS)])


def on_device(
    pair_rep,
    pair_mask,
    ln_in_gain,
    ln_in_bias,
    w_in,
    b_in,
    ln_out_gain,
    ln_out_bias,
    w_out,
    b_out,
    cotangent,
):
    length = pair_rep.shape[1]
    cells = pair_rep.shape[0] * length
    x = pair_rep.reshape(cells, LANES)
    cot = cotangent.reshape(cells, LANES)
    g_in, o_in = ln_in_gain[None], ln_in_bias[None]
    g_out, o_out = ln_out_gain[None], ln_out_bias[None]
    bias_out = b_out[None]

    inputs = (x, pair_mask, g_in, o_in, w_in, b_in)
    sent, pack = call(
        first_kernel, [(8 * LANES, LANES), (cells + 8, LANES)], *inputs, far=len(inputs)
    )
    sides = exchange(sent)
    sides, x_late, pack = lax.optimization_barrier((sides, x, pack))
    back, cg = call(
        side_kernel,
        [(LANES, cells), (cells, LANES)],
        x_late,
        *inputs[2:],
        cot,
        w_out,
        g_out,
        scratch=[(cells, LANES)],
        far=8,
    )
    product = exchange(call(product_kernel, (4 * LANES, LANES), sides))
    packs = [pack, fetch(pack, 1), fetch(pack, 3)]
    across = fetch(packs[1], 1)
    d_product = exchange(call(middle_kernel, (4 * LANES, LANES), product, back))
    update, d_norm, *extras = call(
        update_kernel,
        [(cells, LANES), (cells, LANES)] + [(2 * SHARE, LANES)] * MEMBERS,
        x,
        *inputs[2:],
        cot,
        w_out,
        g_out,
        o_out,
        bias_out,
        product,
        cg,
        far=10,
        scratch=[(cells, LANES), (cells, LANES), (2 * LANES, LANES), (2 * LANES, LANES)],
    )
    factors = functools.partial(
        call,
        outs=[jax.ShapeDtypeStruct((MEMBERS * cells, LANES), jnp.bfloat16)] * 2
        + [(MEMBERS * LANES, cells)],
        scratch=[(LANES, LANES), (LANES, LANES)],
    )
    prelude = (g_in, o_in, w_in, b_in)
    high, low, factor = factors(
        functools.partial(factor_kernel, (0, 1, 3)), args=(*prelude, *packs), far=7
    )
    d_product, high, low, factor, extras, across = lax.optimization_barrier(
        (d_product, high, low, factor, extras, across)
    )
    high, low, factor = factors(
        functools.partial(factor_kernel, (2,)),
        args=(*prelude, across, high, low, factor),
        far=5,
        aliases={5: 0, 6: 1, 7: 2},
    )
    extras = [extras[0]] + [hand(extras[turn], turn) for turn in range(1, MEMBERS)]
    d_sides = exchange(call(back_product_kernel, (8 * LANES, LANES), d_product, sides), PLANE)
    terms = call(weight_kernel, (6 * SHARE, LANES), d_sides, factor, high, low, *extras)
    terms, d_sides = lax.optimization_barrier((terms, d_sides))
    terms = exchange_pairs(terms, PLANE)
    cuts = call(
        cut_kernel,
        [(8 * SHARE, LANES)] * MEMBERS,
        d_sides.reshape(SHARE, 8 * MEMBERS, LANES),
    )
    terms, inputs = lax.optimization_barrier((terms, inputs))
    own = call(
        own_kernel, [(cells, LANES), (cells, LANES), (4 * LANES, cells)], *inputs, far=6, work=10**7,
    )
    cuts = [cuts[0]] + [hand(cuts[turn], turn) for turn in range(1, MEMBERS)]
    grad_pair = call(
        pair_kernel,
        (cells, LANES),
        g_in,
        w_in,
        d_norm,
        *own,
        *cuts,
        scratch=[(8 * LANES, LANES), (8 * LANES, LANES)],
        far=3,
    )
    whole = exchange_pairs(
        call(functools.partial(sum_kernel, length), (6 * LANES, LANES), terms)
    )
    d_win, d_wout = call(last_kernel, [w_in.shape, w_out.shape], whole)
    return (update.reshape(pair_rep.shape), grad_pair.reshape(pair_rep.shape), d_win, d_wout)


def solution(mesh):
    whole = P(PARTS, None, None)
    placed = (whole, P(PARTS, None)) + (P(),) * 8 + (whole,)
    return jax.shard_map(
        on_device,
        mesh=jax.sharding.Mesh(mesh.devices.reshape(SIZES), PARTS),
        in_specs=placed,
        out_specs=(whole, whole, P(), P()),
        check_vma=False,
    )
```

```python
import functools

import jax
import jax.numpy as jnp
from jax import lax
from jax.experimental import pallas as pl
from jax.experimental.pallas import tpu as pltpu
from jax.sharding import PartitionSpec as P

epsilon = 1e-05
LANES = 128
PARTS = ("x_high", "z", "y", "x_low", "core")
SIZES = (2, 4, 4, 2, 2)
AXES = ("x_low", "core", "x_high", "z", "y")
PLANE = AXES[:4]
LINE = "y"
MEMBERS = 4
SHARE = LANES // MEMBERS
F32 = jnp.float32
NN = (((1,), (0,)), ((), ()))
NT = (((1,), (1,)), ((), ()))
TN = (((0,), (0,)), ((), ()))


def mm(a, b, dims):
    return lax.dot_general(
        a, b, dims, precision=lax.Precision.HIGHEST, preferred_element_type=F32
    )


def halves(x):
    high = x.astype(jnp.bfloat16)
    return high, (x - high.astype(F32)).astype(jnp.bfloat16)


def mm3(a, b, dims):
    (a_high, a_low), (b_high, b_low) = halves(a), halves(b)
    ((a_dim,), (b_dim,)), _ = dims
    return lax.dot_general(
        jnp.concatenate([a_high, a_low, a_high], axis=a_dim),
        jnp.concatenate([b_high, b_high, b_low], axis=b_dim),
        dims,
        preferred_element_type=F32,
    )


def every(start, step):
    return pl.ds(start, LANES, stride=step)


def block(b):
    return slice(b * LANES, (b + 1) * LANES)


def column(row):
    return jnp.transpose(jnp.broadcast_to(row, (LANES, LANES)))


def norm_rows(x):
    center = x - jnp.mean(x, -1, keepdims=True)
    scale = lax.rsqrt(jnp.mean(center * center, -1, keepdims=True) + epsilon)
    return center * scale, scale


def norm_cols(x):
    center = x - jnp.mean(x, 0, keepdims=True)
    scale = lax.rsqrt(jnp.mean(center * center, 0, keepdims=True) + epsilon)
    return center * scale, scale


def places():
    s = lax.broadcasted_iota(jnp.int32, (LANES, LANES), 0)
    d = lax.broadcasted_iota(jnp.int32, (LANES, LANES), 1)
    x_low_core, x_high, z, y = s // 32, (s // 16) % 2, (s // 4) % 4, s % 4
    return (d == x_high * 64 + z * 16 + y * 4 + x_low_core).astype(F32)


def project(normed, w_ref, b_ref, part, mul=mm):
    return mul(jnp.transpose(w_ref[:, block(part)]), normed, NT) + jnp.tile(
        column(b_ref[pl.ds(part * LANES, LANES)][None]), (1, normed.shape[0] // LANES)
    )


def cell_mask(mask_ref):
    mask = mask_ref[...].astype(F32)
    return jnp.concatenate([mask[0:1], mask[1:2]], axis=1)


def first_kernel(x_ref, mask_ref, g_ref, b_ref, w_ref, bin_ref, out_ref, pack_ref):
    hat, _ = norm_rows(x_ref[...])
    normed = hat * g_ref[...] + b_ref[...]
    mask = cell_mask(mask_ref)
    weights = jnp.concatenate([jnp.transpose(w_ref[:, block(p)]) for p in range(4)], axis=0)
    bias = jnp.concatenate(
        [column(bin_ref[pl.ds(p * LANES, LANES)][None]) for p in range(4)], axis=0
    )
    pieces = mm3(weights, normed, NT) + jnp.tile(bias, (1, 4))
    for side in range(2):
        value = mask * jax.nn.sigmoid(pieces[block(2 * side)]) * pieces[block(2 * side + 1)]
        for b in range(4):
            out_ref[every(4 * side + b, 8), :] = value[:, block(b)]
    pack_ref[0 : 4 * LANES, :] = x_ref[...]
    pack_ref[4 * LANES : 4 * LANES + 8, :] = jnp.concatenate(
        [mask[:, block(b)] for b in range(4)] + [jnp.zeros((4, LANES), F32)], axis=0
    )


def side_kernel(
    x_ref, g_ref, b_ref, w_ref, bin_ref, cot_ref, wout_ref, gout_ref, back_ref, cg_ref, held_ref,
):
    hat, _ = norm_rows(x_ref[...])
    normed = hat * g_ref[...] + b_ref[...]
    held_ref[...] = cot_ref[...] * gate_of(normed, w_ref, bin_ref)
    cg = mm(places(), in_quarters(held_ref), NN)
    for q in range(4):
        cg_ref[block(q), :] = cg[:, block(q)]
    back_ref[...] = jnp.tile(column(gout_ref[...]), (1, 4)) * mm3(wout_ref[...], cg_ref[...], NT)


def quarter(q):
    return every((q // 2) * 256 + q % 2, 2)


def in_quarters(ref):
    return jnp.concatenate([ref[quarter(q), :] for q in range(4)], axis=1)


def gate_of(normed, w_ref, bin_ref):
    return jax.nn.sigmoid(
        mm3(normed, w_ref[:, block(4)], NN) + bin_ref[pl.ds(4 * LANES, LANES)][None]
    )


def gather_sides(in_ref):
    sides = []
    for side in range(2):
        rows = [
            jnp.concatenate([in_ref[every(4 * side + 2 * r + h, 8), :] for h in range(2)], axis=1)
            for r in range(2)
        ]
        sides.append(jnp.concatenate(rows, axis=0))
    return sides


def product_kernel(in_ref, out_ref):
    left, right = gather_sides(in_ref)
    product = mm3(left, right, NT)
    for q in range(4):
        out_ref[every(q, 4), :] = product[block(q // 2), block(q % 2)]


def middle_kernel(in_ref, back_ref, out_ref):
    for q in range(4):
        hat, scale = norm_cols(in_ref[every(q, 4), :])
        back = back_ref[:, block(q)]
        first = jnp.mean(back, 0, keepdims=True)
        second = jnp.mean(back * hat, 0, keepdims=True)
        out_ref[every(q, 4), :] = scale * (back - first - hat * second)


def update_kernel(
    x_ref, g_ref, b_ref, w_ref, bin_ref, cot_ref, wout_ref, gout_ref, boff_ref, bout_ref,
    in_ref, cg_ref,
    update_ref, dnorm_ref, *rest,
):
    extra_refs, (open_ref, gate_ref, grads_ref, held_ref) = rest[:MEMBERS], rest[MEMBERS:]
    hat, _ = norm_rows(x_ref[...])
    normed = hat * g_ref[...] + b_ref[...]
    gate_ref[...] = gate_of(normed, w_ref, bin_ref)
    gain, bias = column(gout_ref[...]), column(boff_ref[...])
    normed_product = jnp.concatenate(
        [norm_cols(in_ref[every(q, 4), :])[0] * gain + bias for q in range(4)], axis=1
    )
    grads_ref[block(0), :] = mm3(normed_product, cg_ref[...], NN)
    projected = mm3(jnp.transpose(normed_product), wout_ref[...], NN)
    projected = jnp.concatenate([projected[block(q), :] for q in range(4)], axis=1)
    projected = mm(places(), projected, TN)
    for q in range(4):
        open_ref[quarter(q), :] = projected[:, block(q)] + bout_ref[...]
    gate = gate_ref[...]
    projected = open_ref[...]
    update_ref[...] = gate * projected
    d_open = cot_ref[...] * projected * gate * (1.0 - gate)
    grads_ref[block(1), :] = mm3(jnp.transpose(normed), d_open, NN)
    dnorm_ref[...] = mm3(d_open, w_ref[:, block(4)], NT)
    for member in range(MEMBERS):
        for part in range(2):
            held_ref[share(2 * member + part), :] = grads_ref[
                pl.ds(part * LANES + member, SHARE, stride=MEMBERS), :
            ]
    for turn in range(MEMBERS):
        extra_refs[turn][...] = held_ref[pl.ds(member_at(turn) * 2 * SHARE, 2 * SHARE), :]


def member_at(turn):
    return lax.rem(lax.axis_index(LINE) + turn, MEMBERS)


def share(n):
    return slice(n * SHARE, (n + 1) * SHARE)


def mine():
    u = lax.broadcasted_iota(jnp.int32, (SHARE, LANES), 0)
    f = lax.broadcasted_iota(jnp.int32, (SHARE, LANES), 1)
    return (f == u * MEMBERS + lax.axis_index(LINE)).astype(F32)


def my_weights(pick, w_ref):
    return jnp.concatenate([mm(pick, w_ref[:, block(p)], NT) for p in range(4)], axis=0)


def factor_kernel(turns, g_ref, b_ref, w_ref, bin_ref, *refs):
    packs, (high_ref, low_ref, factor_ref, weights_ref, bias_ref) = refs[: len(turns)], refs[-5:]
    pick = mine()
    weights_ref[...] = my_weights(pick, w_ref)
    for p in range(4):
        row = bin_ref[pl.ds(p * LANES, LANES)][None]
        bias_ref[share(p), :] = jnp.broadcast_to(
            jnp.sum(pick * row, axis=1, keepdims=True), (SHARE, LANES)
        )
    for pack, turn in zip(packs, turns):
        hat, _ = norm_rows(pack[0 : 4 * LANES, :])
        normed = hat * g_ref[...] + b_ref[...]
        member = member_at(turn)
        rows = pl.ds(pl.multiple_of(member * 4 * LANES, 4 * LANES), 4 * LANES)
        high_ref[rows, :], low_ref[rows, :] = halves(normed)
        pieces = mm3(weights_ref[...], normed, NT) + jnp.tile(bias_ref[...], (1, 4))
        mask = jnp.concatenate([pack[4 * LANES + b : 4 * LANES + b + 1, :] for b in range(4)], axis=1)
        parts = []
        for side in range(2):
            sig = jax.nn.sigmoid(pieces[share(2 * side)])
            open_part = mask * sig
            parts += [open_part * (1.0 - sig) * pieces[share(2 * side + 1)], open_part]
        factor_ref[pl.ds(member * LANES, LANES), :] = jnp.concatenate(parts, axis=0)


def back_product_kernel(grad_ref, in_ref, out_ref):
    left, right = gather_sides(in_ref)
    grad = jnp.concatenate(
        [
            jnp.concatenate([grad_ref[every(2 * r + c, 4), :] for c in range(2)], axis=1)
            for r in range(2)
        ],
        axis=0,
    )
    sides = (mm3(grad, right, NN), mm3(jnp.transpose(grad), left, NN))
    for side in range(2):
        for b in range(4):
            out_ref[every(4 * side + b, 8), :] = sides[side][block(b // 2), block(b % 2)]


def piece_grads(in_ref, factor_ref, member):
    parts = []
    for side in range(2):
        grad = jnp.concatenate(
            [
                in_ref[pl.ds(member * 8 + 4 * side + b, SHARE, stride=8 * MEMBERS), :]
                for b in range(4)
            ],
            axis=1,
        )
        parts += [grad * factor_ref[share(4 * member + 2 * side + m), :] for m in range(2)]
    return jnp.concatenate(parts, axis=0)


def weight_kernel(in_ref, factor_ref, high_ref, low_ref, *refs):
    extras, out_ref = refs[:MEMBERS], refs[MEMBERS]
    grads = jnp.concatenate([piece_grads(in_ref, factor_ref, m) for m in range(MEMBERS)], axis=1)
    high, low = halves(grads)
    terms = sum(
        lax.dot_general(a, b[...], NN, preferred_element_type=F32)
        for a, b in ((high, high_ref), (low, high_ref), (high, low_ref))
    )
    extra = (extras[0][...] + extras[1][...]) + (extras[2][...] + extras[3][...])
    for part in range(4):
        out_ref[pl.ds(part, SHARE, stride=6), :] = terms[share(part), :]
    for part in range(2):
        out_ref[pl.ds(4 + part, SHARE, stride=6), :] = extra[share(part), :]


def cut_kernel(in_ref, *outs):
    for turn in range(MEMBERS):
        first = pl.multiple_of(member_at(turn) * 8, 8)
        rows = in_ref[:, pl.ds(first, 8), :]
        outs[turn][...] = rows.reshape(outs[turn].shape)


def own_kernel(x_ref, mask_ref, g_ref, b_ref, w_ref, bin_ref, hat_ref, scale_ref, factor_ref):
    hat, scale = norm_rows(x_ref[...])
    hat_ref[...] = hat
    scale_ref[...] = jnp.broadcast_to(scale, hat.shape)
    normed = hat * g_ref[...] + b_ref[...]
    mask = cell_mask(mask_ref)
    for side in range(2):
        sig = jax.nn.sigmoid(project(normed, w_ref, bin_ref, 2 * side, mm3))
        value = project(normed, w_ref, bin_ref, 2 * side + 1, mm3)
        open_part = mask * sig
        factor_ref[block(2 * side), :] = open_part * (1.0 - sig) * value
        factor_ref[block(2 * side + 1), :] = open_part


def pair_kernel(
    g_ref, w_ref, dnorm_ref, hat_ref, scale_ref, factor_ref, *refs
):
    cuts, (out_ref, held_ref, sides_ref) = refs[:MEMBERS], refs[MEMBERS:]
    size = 8 * SHARE
    for turn in range(MEMBERS):
        held_ref[pl.ds(member_at(MEMBERS - turn) * size, size), :] = cuts[turn][...]
    for member in range(MEMBERS):
        for n in range(8):
            sides_ref[pl.ds(n * LANES + member, SHARE, stride=MEMBERS), :] = held_ref[
                pl.ds(member * size + n, SHARE, stride=8), :
            ]
    parts = []
    for side in range(2):
        grad = jnp.concatenate([sides_ref[block(4 * side + b), :] for b in range(4)], axis=1)
        parts += [grad * factor_ref[block(2 * side + m), :] for m in range(2)]
    d_normed = mm3(w_ref[:, : 4 * LANES], jnp.concatenate(parts, axis=0), NN)
    d_normed = jnp.transpose(d_normed) + dnorm_ref[...]
    hat = hat_ref[...]
    d_hat = d_normed * g_ref[...]
    first = jnp.mean(d_hat, -1, keepdims=True)
    second = jnp.mean(d_hat * hat, -1, keepdims=True)
    out_ref[...] = scale_ref[...] * (d_hat - first - hat * second)


def sum_kernel(length, in_ref, out_ref):
    terms = in_ref[...]
    total = jnp.sum(terms.reshape(SHARE // 4, 24, LANES), 0)
    mine = (total[0:6] + total[6:12]) + (total[12:18] + total[18:24])
    mine = jnp.concatenate([mine] * 4, axis=0) * (1.0 / length)
    out_ref[...] = jnp.broadcast_to(mine[None], (LANES // 4, 24, LANES)).reshape(out_ref.shape)


def last_kernel(in_ref, win_ref, wout_ref):
    for part in range(4):
        win_ref[:, block(part)] = jnp.transpose(in_ref[every(part, 6), :])
    wout_ref[...] = in_ref[every(4, 6), :]
    win_ref[:, block(4)] = in_ref[every(5, 6), :]


def call(kernel, outs, *given, args=(), scratch=(), far=0, work=0, aliases={}):
    args = (*given, *args)
    many = isinstance(outs, list)
    shapes = [
        jax.ShapeDtypeStruct(s, F32) if isinstance(s, tuple) else s
        for s in (outs if many else [outs])
    ]
    near = pl.BlockSpec(memory_space=pltpu.VMEM)
    held = [pltpu.VMEM(a.shape, a.dtype) for a in args[:far]]

    def body(*refs):
        end = len(args) + len(shapes)
        places = refs[end : end + far]
        copies = [
            pltpu.make_async_copy(refs[n], places[n], refs[-1].at[n]) for n in range(far)
        ]
        for copy in copies:
            copy.start()
        for copy in copies:
            copy.wait()
        kernel(*places, *refs[far:end], *refs[end + far : len(refs) - 1])

    return pl.pallas_call(
        body if far else kernel,
        out_shape=shapes if many else shapes[0],
        in_specs=[pl.BlockSpec(memory_space=pltpu.HBM)] * far + [near] * (len(args) - far),
        out_specs=[near] * len(shapes) if many else near,
        scratch_shapes=held
        + [pltpu.VMEM(s, F32) for s in scratch]
        + ([pltpu.SemaphoreType.DMA((far,))] if far else []),
        input_output_aliases=aliases,
        cost_estimate=pl.CostEstimate(flops=1000 * work, transcendentals=0, bytes_accessed=work)
        if work
        else None,
        compiler_params=pltpu.CompilerParams(vmem_limit_bytes=24 * 2**20),
    )(*[pltpu.with_memory_space_constraint(a, pltpu.HBM) for a in args[:far]], *args[far:])


def exchange(x, axes=AXES):
    return lax.all_to_all(x, axes, split_axis=0, concat_axis=0, tiled=True)


def exchange_pairs(x, axes=AXES):
    return exchange(x.reshape(-1, 2, LANES), axes).reshape(x.shape)


def fetch(x, turn):
    return lax.ppermute(x, LINE, [((n + turn) % MEMBERS, n) for n in range(MEMBERS)])


def hand(x, turn):
    return lax.ppermute(x, LINE, [(n, (n + turn) % MEMBERS) for n in range(MEMBERS)])


def on_device(
    pair_rep,
    pair_mask,
    ln_in_gain,
    ln_in_bias,
    w_in,
    b_in,
    ln_out_gain,
    ln_out_bias,
    w_out,
    b_out,
    cotangent,
):
    length = pair_rep.shape[1]
    cells = pair_rep.shape[0] * length
    x = pair_rep.reshape(cells, LANES)
    cot = cotangent.reshape(cells, LANES)
    g_in, o_in = ln_in_gain[None], ln_in_bias[None]
    g_out, o_out = ln_out_gain[None], ln_out_bias[None]
    bias_out = b_out[None]

    inputs = (x, pair_mask, g_in, o_in, w_in, b_in)
    sent, pack = call(
        first_kernel, [(8 * LANES, LANES), (cells + 8, LANES)], *inputs, far=len(inputs)
    )
    next_pack, last_pack = fetch(pack, 1), fetch(pack, 3)
    sides = exchange(sent)
    sides, x_late, pack = lax.optimization_barrier((sides, x, pack))
    back, cg = call(
        side_kernel,
        [(LANES, cells), (cells, LANES)],
        x_late,
        *inputs[2:],
        cot,
        w_out,
        g_out,
        scratch=[(cells, LANES)],
        far=8,
    )
    product = exchange(call(product_kernel, (4 * LANES, LANES), sides))
    packs = [pack, next_pack, last_pack]
    across = fetch(packs[1], 1)
    d_product = exchange(call(middle_kernel, (4 * LANES, LANES), product, back))
    update, d_norm, *extras = call(
        update_kernel,
        [(cells, LANES), (cells, LANES)] + [(2 * SHARE, LANES)] * MEMBERS,
        x,
        *inputs[2:],
        cot,
        w_out,
        g_out,
        o_out,
        bias_out,
        product,
        cg,
        far=10,
        scratch=[(cells, LANES), (cells, LANES), (2 * LANES, LANES), (2 * LANES, LANES)],
    )
    factors = functools.partial(
        call,
        outs=[jax.ShapeDtypeStruct((MEMBERS * cells, LANES), jnp.bfloat16)] * 2
        + [(MEMBERS * LANES, cells)],
        scratch=[(LANES, LANES), (LANES, LANES)],
    )
    prelude = (g_in, o_in, w_in, b_in)
    high, low, factor = factors(
        functools.partial(factor_kernel, (0, 1, 3)), args=(*prelude, *packs), far=7
    )
    d_product, high, low, factor, extras, across = lax.optimization_barrier(
        (d_product, high, low, factor, extras, across)
    )
    high, low, factor = factors(
        functools.partial(factor_kernel, (2,)),
        args=(*prelude, across, high, low, factor),
        far=5,
        aliases={5: 0, 6: 1, 7: 2},
    )
    extras = [extras[0]] + [hand(extras[turn], turn) for turn in range(1, MEMBERS)]
    d_sides = exchange(call(back_product_kernel, (8 * LANES, LANES), d_product, sides), PLANE)
    terms = call(weight_kernel, (6 * SHARE, LANES), d_sides, factor, high, low, *extras)
    terms, d_sides = lax.optimization_barrier((terms, d_sides))
    terms = exchange_pairs(terms, PLANE)
    cuts = call(
        cut_kernel,
        [(8 * SHARE, LANES)] * MEMBERS,
        d_sides.reshape(SHARE, 8 * MEMBERS, LANES),
    )
    terms, inputs = lax.optimization_barrier((terms, inputs))
    own = call(
        own_kernel, [(cells, LANES), (cells, LANES), (4 * LANES, cells)], *inputs, far=6, work=10**7,
    )
    cuts = [cuts[0]] + [hand(cuts[turn], turn) for turn in range(1, MEMBERS)]
    grad_pair = call(
        pair_kernel,
        (cells, LANES),
        g_in,
        w_in,
        d_norm,
        *own,
        *cuts,
        scratch=[(8 * LANES, LANES), (8 * LANES, LANES)],
        far=3,
    )
    whole = exchange_pairs(
        call(functools.partial(sum_kernel, length), (6 * LANES, LANES), terms)
    )
    d_win, d_wout = call(last_kernel, [w_in.shape, w_out.shape], whole)
    return (update.reshape(pair_rep.shape), grad_pair.reshape(pair_rep.shape), d_win, d_wout)


def solution(mesh):
    whole = P(PARTS, None, None)
    placed = (whole, P(PARTS, None)) + (P(),) * 8 + (whole,)
    return jax.shard_map(
        on_device,
        mesh=jax.sharding.Mesh(mesh.devices.reshape(SIZES), PARTS),
        in_specs=placed,
        out_specs=(whole, whole, P(), P()),
        check_vma=False,
    )
```

```python
import functools

import jax
import jax.numpy as jnp
from jax import lax
from jax.experimental import pallas as pl
from jax.experimental.pallas import tpu as pltpu
from jax.sharding import PartitionSpec as P

epsilon = 1e-05
LANES = 128
PARTS = ("x_high", "z", "y", "x_low", "core")
SIZES = (2, 4, 4, 2, 2)
AXES = ("x_low", "core", "x_high", "z", "y")
PLANE = AXES[:4]
LINE = "y"
MEMBERS = 4
SHARE = LANES // MEMBERS
F32 = jnp.float32
NN = (((1,), (0,)), ((), ()))
NT = (((1,), (1,)), ((), ()))
TN = (((0,), (0,)), ((), ()))


def mm(a, b, dims):
    return lax.dot_general(
        a, b, dims, precision=lax.Precision.HIGHEST, preferred_element_type=F32
    )


def halves(x):
    high = x.astype(jnp.bfloat16)
    return high, (x - high.astype(F32)).astype(jnp.bfloat16)


def mm3(a, b, dims):
    (a_high, a_low), (b_high, b_low) = halves(a), halves(b)
    ((a_dim,), (b_dim,)), _ = dims
    return lax.dot_general(
        jnp.concatenate([a_high, a_low, a_high], axis=a_dim),
        jnp.concatenate([b_high, b_high, b_low], axis=b_dim),
        dims,
        preferred_element_type=F32,
    )


def every(start, step):
    return pl.ds(start, LANES, stride=step)


def block(b):
    return slice(b * LANES, (b + 1) * LANES)


def column(row):
    return jnp.transpose(jnp.broadcast_to(row, (LANES, LANES)))


def norm_rows(x):
    center = x - jnp.mean(x, -1, keepdims=True)
    scale = lax.rsqrt(jnp.mean(center * center, -1, keepdims=True) + epsilon)
    return center * scale, scale


def norm_cols(x):
    center = x - jnp.mean(x, 0, keepdims=True)
    scale = lax.rsqrt(jnp.mean(center * center, 0, keepdims=True) + epsilon)
    return center * scale, scale


def places():
    s = lax.broadcasted_iota(jnp.int32, (LANES, LANES), 0)
    d = lax.broadcasted_iota(jnp.int32, (LANES, LANES), 1)
    x_low_core, x_high, z, y = s // 32, (s // 16) % 2, (s // 4) % 4, s % 4
    return (d == x_high * 64 + z * 16 + y * 4 + x_low_core).astype(F32)


def project(normed, w_ref, b_ref, part, mul=mm):
    return mul(jnp.transpose(w_ref[:, block(part)]), normed, NT) + jnp.tile(
        column(b_ref[pl.ds(part * LANES, LANES)][None]), (1, normed.shape[0] // LANES)
    )


def cell_mask(mask_ref):
    mask = mask_ref[...].astype(F32)
    return jnp.concatenate([mask[0:1], mask[1:2]], axis=1)


def first_kernel(x_ref, mask_ref, g_ref, b_ref, w_ref, bin_ref, out_ref, pack_ref):
    hat, _ = norm_rows(x_ref[...])
    normed = hat * g_ref[...] + b_ref[...]
    mask = cell_mask(mask_ref)
    weights = jnp.concatenate([jnp.transpose(w_ref[:, block(p)]) for p in range(4)], axis=0)
    bias = jnp.concatenate(
        [column(bin_ref[pl.ds(p * LANES, LANES)][None]) for p in range(4)], axis=0
    )
    pieces = mm3(weights, normed, NT) + jnp.tile(bias, (1, 4))
    for side in range(2):
        value = mask * jax.nn.sigmoid(pieces[block(2 * side)]) * pieces[block(2 * side + 1)]
        for b in range(4):
            out_ref[every(4 * side + b, 8), :] = value[:, block(b)]
    pack_ref[0 : 4 * LANES, :] = x_ref[...]
    pack_ref[4 * LANES : 4 * LANES + 8, :] = jnp.concatenate(
        [mask[:, block(b)] for b in range(4)] + [jnp.zeros((4, LANES), F32)], axis=0
    )


def side_kernel(
    x_ref, g_ref, b_ref, w_ref, bin_ref, cot_ref, wout_ref, gout_ref, back_ref, cg_ref, held_ref,
):
    hat, _ = norm_rows(x_ref[...])
    normed = hat * g_ref[...] + b_ref[...]
    held_ref[...] = cot_ref[...] * gate_of(normed, w_ref, bin_ref)
    cg = mm(places(), in_quarters(held_ref), NN)
    for q in range(4):
        cg_ref[block(q), :] = cg[:, block(q)]
    back_ref[...] = jnp.tile(column(gout_ref[...]), (1, 4)) * mm3(wout_ref[...], cg_ref[...], NT)


def quarter(q):
    return every((q // 2) * 256 + q % 2, 2)


def in_quarters(ref):
    return jnp.concatenate([ref[quarter(q), :] for q in range(4)], axis=1)


def gate_of(normed, w_ref, bin_ref):
    return jax.nn.sigmoid(
        mm3(normed, w_ref[:, block(4)], NN) + bin_ref[pl.ds(4 * LANES, LANES)][None]
    )


def gather_sides(in_ref):
    sides = []
    for side in range(2):
        rows = [
            jnp.concatenate([in_ref[every(4 * side + 2 * r + h, 8), :] for h in range(2)], axis=1)
            for r in range(2)
        ]
        sides.append(jnp.concatenate(rows, axis=0))
    return sides


def product_kernel(in_ref, out_ref):
    left, right = gather_sides(in_ref)
    product = mm3(left, right, NT)
    for q in range(4):
        out_ref[every(q, 4), :] = product[block(q // 2), block(q % 2)]


def middle_kernel(in_ref, back_ref, out_ref):
    for q in range(4):
        hat, scale = norm_cols(in_ref[every(q, 4), :])
        back = back_ref[:, block(q)]
        first = jnp.mean(back, 0, keepdims=True)
        second = jnp.mean(back * hat, 0, keepdims=True)
        out_ref[every(q, 4), :] = scale * (back - first - hat * second)


def update_kernel(
    x_ref, g_ref, b_ref, w_ref, bin_ref, cot_ref, wout_ref, gout_ref, boff_ref, bout_ref,
    in_ref, cg_ref,
    update_ref, dnorm_ref, *rest,
):
    extra_refs, (open_ref, gate_ref, grads_ref, held_ref) = rest[:MEMBERS], rest[MEMBERS:]
    hat, _ = norm_rows(x_ref[...])
    normed = hat * g_ref[...] + b_ref[...]
    gate_ref[...] = gate_of(normed, w_ref, bin_ref)
    gain, bias = column(gout_ref[...]), column(boff_ref[...])
    normed_product = jnp.concatenate(
        [norm_cols(in_ref[every(q, 4), :])[0] * gain + bias for q in range(4)], axis=1
    )
    grads_ref[block(0), :] = mm3(normed_product, cg_ref[...], NN)
    projected = mm3(jnp.transpose(normed_product), wout_ref[...], NN)
    projected = jnp.concatenate([projected[block(q), :] for q in range(4)], axis=1)
    projected = mm(places(), projected, TN)
    for q in range(4):
        open_ref[quarter(q), :] = projected[:, block(q)] + bout_ref[...]
    gate = gate_ref[...]
    projected = open_ref[...]
    update_ref[...] = gate * projected
    d_open = cot_ref[...] * projected * gate * (1.0 - gate)
    grads_ref[block(1), :] = mm3(jnp.transpose(normed), d_open, NN)
    dnorm_ref[...] = mm3(d_open, w_ref[:, block(4)], NT)
    for member in range(MEMBERS):
        for part in range(2):
            held_ref[share(2 * member + part), :] = grads_ref[
                pl.ds(part * LANES + member, SHARE, stride=MEMBERS), :
            ]
    for turn in range(MEMBERS):
        extra_refs[turn][...] = held_ref[pl.ds(member_at(turn) * 2 * SHARE, 2 * SHARE), :]


def member_at(turn):
    return lax.rem(lax.axis_index(LINE) + turn, MEMBERS)


def share(n):
    return slice(n * SHARE, (n + 1) * SHARE)


def mine():
    u = lax.broadcasted_iota(jnp.int32, (SHARE, LANES), 0)
    f = lax.broadcasted_iota(jnp.int32, (SHARE, LANES), 1)
    return (f == u * MEMBERS + lax.axis_index(LINE)).astype(F32)


def my_weights(pick, w_ref):
    return jnp.concatenate([mm(pick, w_ref[:, block(p)], NT) for p in range(4)], axis=0)


def factor_kernel(turns, g_ref, b_ref, w_ref, bin_ref, *refs):
    packs, (high_ref, low_ref, factor_ref, weights_ref, bias_ref) = refs[: len(turns)], refs[-5:]
    pick = mine()
    weights_ref[...] = my_weights(pick, w_ref)
    for p in range(4):
        row = bin_ref[pl.ds(p * LANES, LANES)][None]
        bias_ref[share(p), :] = jnp.broadcast_to(
            jnp.sum(pick * row, axis=1, keepdims=True), (SHARE, LANES)
        )
    for pack, turn in zip(packs, turns):
        hat, _ = norm_rows(pack[0 : 4 * LANES, :])
        normed = hat * g_ref[...] + b_ref[...]
        member = member_at(turn)
        rows = pl.ds(pl.multiple_of(member * 4 * LANES, 4 * LANES), 4 * LANES)
        high_ref[rows, :], low_ref[rows, :] = halves(normed)
        pieces = mm3(weights_ref[...], normed, NT) + jnp.tile(bias_ref[...], (1, 4))
        mask = jnp.concatenate([pack[4 * LANES + b : 4 * LANES + b + 1, :] for b in range(4)], axis=1)
        parts = []
        for side in range(2):
            sig = jax.nn.sigmoid(pieces[share(2 * side)])
            open_part = mask * sig
            parts += [open_part * (1.0 - sig) * pieces[share(2 * side + 1)], open_part]
        factor_ref[pl.ds(member * LANES, LANES), :] = jnp.concatenate(parts, axis=0)


def back_product_kernel(grad_ref, in_ref, out_ref):
    left, right = gather_sides(in_ref)
    grad = jnp.concatenate(
        [
            jnp.concatenate([grad_ref[every(2 * r + c, 4), :] for c in range(2)], axis=1)
            for r in range(2)
        ],
        axis=0,
    )
    sides = (mm3(grad, right, NN), mm3(jnp.transpose(grad), left, NN))
    for side in range(2):
        for b in range(4):
            out_ref[every(4 * side + b, 8), :] = sides[side][block(b // 2), block(b % 2)]


def piece_grads(in_ref, factor_ref, member):
    parts = []
    for side in range(2):
        grad = jnp.concatenate(
            [
                in_ref[pl.ds(member * 8 + 4 * side + b, SHARE, stride=8 * MEMBERS), :]
                for b in range(4)
            ],
            axis=1,
        )
        parts += [grad * factor_ref[share(4 * member + 2 * side + m), :] for m in range(2)]
    return jnp.concatenate(parts, axis=0)


def weight_kernel(in_ref, factor_ref, high_ref, low_ref, *refs):
    extras, out_ref = refs[:MEMBERS], refs[MEMBERS]
    grads = jnp.concatenate([piece_grads(in_ref, factor_ref, m) for m in range(MEMBERS)], axis=1)
    high, low = halves(grads)
    terms = sum(
        lax.dot_general(a, b[...], NN, preferred_element_type=F32)
        for a, b in ((high, high_ref), (low, high_ref), (high, low_ref))
    )
    extra = (extras[0][...] + extras[1][...]) + (extras[2][...] + extras[3][...])
    for part in range(4):
        out_ref[pl.ds(part, SHARE, stride=6), :] = terms[share(part), :]
    for part in range(2):
        out_ref[pl.ds(4 + part, SHARE, stride=6), :] = extra[share(part), :]


def cut_kernel(in_ref, *outs):
    for turn in range(MEMBERS):
        first = pl.multiple_of(member_at(turn) * 8, 8)
        rows = in_ref[:, pl.ds(first, 8), :]
        outs[turn][...] = rows.reshape(outs[turn].shape)


def own_kernel(x_ref, mask_ref, g_ref, b_ref, w_ref, bin_ref, hat_ref, scale_ref, factor_ref):
    hat, scale = norm_rows(x_ref[...])
    hat_ref[...] = hat
    scale_ref[...] = jnp.broadcast_to(scale, hat.shape)
    normed = hat * g_ref[...] + b_ref[...]
    mask = cell_mask(mask_ref)
    for side in range(2):
        sig = jax.nn.sigmoid(project(normed, w_ref, bin_ref, 2 * side, mm3))
        value = project(normed, w_ref, bin_ref, 2 * side + 1, mm3)
        open_part = mask * sig
        factor_ref[block(2 * side), :] = open_part * (1.0 - sig) * value
        factor_ref[block(2 * side + 1), :] = open_part


def pair_kernel(
    g_ref, w_ref, dnorm_ref, hat_ref, scale_ref, factor_ref, *refs
):
    cuts, (out_ref, held_ref, sides_ref) = refs[:MEMBERS], refs[MEMBERS:]
    size = 8 * SHARE
    for turn in range(MEMBERS):
        held_ref[pl.ds(member_at(MEMBERS - turn) * size, size), :] = cuts[turn][...]
    for member in range(MEMBERS):
        for n in range(8):
            sides_ref[pl.ds(n * LANES + member, SHARE, stride=MEMBERS), :] = held_ref[
                pl.ds(member * size + n, SHARE, stride=8), :
            ]
    parts = []
    for side in range(2):
        grad = jnp.concatenate([sides_ref[block(4 * side + b), :] for b in range(4)], axis=1)
        parts += [grad * factor_ref[block(2 * side + m), :] for m in range(2)]
    d_normed = mm3(w_ref[:, : 4 * LANES], jnp.concatenate(parts, axis=0), NN)
    d_normed = jnp.transpose(d_normed) + dnorm_ref[...]
    hat = hat_ref[...]
    d_hat = d_normed * g_ref[...]
    first = jnp.mean(d_hat, -1, keepdims=True)
    second = jnp.mean(d_hat * hat, -1, keepdims=True)
    out_ref[...] = scale_ref[...] * (d_hat - first - hat * second)


def sum_kernel(length, in_ref, out_ref):
    terms = in_ref[...]
    total = jnp.sum(terms.reshape(SHARE // 4, 24, LANES), 0)
    mine = (total[0:6] + total[6:12]) + (total[12:18] + total[18:24])
    mine = jnp.concatenate([mine] * 4, axis=0) * (1.0 / length)
    out_ref[...] = jnp.broadcast_to(mine[None], (LANES // 4, 24, LANES)).reshape(out_ref.shape)


def last_kernel(in_ref, win_ref, wout_ref, win_held, wout_held, sems):
    copies = [
        pltpu.make_async_copy(win_held.at[:, block(p)], win_ref.at[:, block(p)], sems.at[p])
        for p in range(5)
    ] + [pltpu.make_async_copy(wout_held, wout_ref, sems.at[5])]
    wout_held[...] = in_ref[every(4, 6), :]
    copies[5].start()
    win_held[:, block(4)] = in_ref[every(5, 6), :]
    copies[4].start()
    for part in range(4):
        win_held[:, block(part)] = jnp.transpose(in_ref[every(part, 6), :])
        copies[part].start()
    for copy in copies:
        copy.wait()


def call(kernel, outs, *given, args=(), scratch=(), far=0, work=0, aliases={}):
    args = (*given, *args)
    many = isinstance(outs, list)
    shapes = [
        jax.ShapeDtypeStruct(s, F32) if isinstance(s, tuple) else s
        for s in (outs if many else [outs])
    ]
    near = pl.BlockSpec(memory_space=pltpu.VMEM)
    held = [pltpu.VMEM(a.shape, a.dtype) for a in args[:far]]

    def body(*refs):
        end = len(args) + len(shapes)
        places = refs[end : end + far]
        copies = [
            pltpu.make_async_copy(refs[n], places[n], refs[-1].at[n]) for n in range(far)
        ]
        for copy in copies:
            copy.start()
        for copy in copies:
            copy.wait()
        kernel(*places, *refs[far:end], *refs[end + far : len(refs) - 1])

    return pl.pallas_call(
        body if far else kernel,
        out_shape=shapes if many else shapes[0],
        in_specs=[pl.BlockSpec(memory_space=pltpu.HBM)] * far + [near] * (len(args) - far),
        out_specs=[near] * len(shapes) if many else near,
        scratch_shapes=held
        + [pltpu.VMEM(s, F32) for s in scratch]
        + ([pltpu.SemaphoreType.DMA((far,))] if far else []),
        input_output_aliases=aliases,
        cost_estimate=pl.CostEstimate(flops=1000 * work, transcendentals=0, bytes_accessed=work)
        if work
        else None,
        compiler_params=pltpu.CompilerParams(vmem_limit_bytes=24 * 2**20),
    )(*[pltpu.with_memory_space_constraint(a, pltpu.HBM) for a in args[:far]], *args[far:])


def exchange(x, axes=AXES):
    return lax.all_to_all(x, axes, split_axis=0, concat_axis=0, tiled=True)


def exchange_pairs(x, axes=AXES):
    return exchange(x.reshape(-1, 2, LANES), axes).reshape(x.shape)


def fetch(x, turn):
    return lax.ppermute(x, LINE, [((n + turn) % MEMBERS, n) for n in range(MEMBERS)])


def hand(x, turn):
    return lax.ppermute(x, LINE, [(n, (n + turn) % MEMBERS) for n in range(MEMBERS)])


def on_device(
    pair_rep,
    pair_mask,
    ln_in_gain,
    ln_in_bias,
    w_in,
    b_in,
    ln_out_gain,
    ln_out_bias,
    w_out,
    b_out,
    cotangent,
):
    length = pair_rep.shape[1]
    cells = pair_rep.shape[0] * length
    x = pair_rep.reshape(cells, LANES)
    cot = cotangent.reshape(cells, LANES)
    g_in, o_in = ln_in_gain[None], ln_in_bias[None]
    g_out, o_out = ln_out_gain[None], ln_out_bias[None]
    bias_out = b_out[None]

    inputs = (x, pair_mask, g_in, o_in, w_in, b_in)
    sent, pack = call(
        first_kernel, [(8 * LANES, LANES), (cells + 8, LANES)], *inputs, far=len(inputs)
    )
    next_pack, last_pack = fetch(pack, 1), fetch(pack, 3)
    sides = exchange(sent)
    sides, x_late, pack = lax.optimization_barrier((sides, x, pack))
    back, cg = call(
        side_kernel,
        [(LANES, cells), (cells, LANES)],
        x_late,
        *inputs[2:],
        cot,
        w_out,
        g_out,
        scratch=[(cells, LANES)],
        far=8,
    )
    product = exchange(call(product_kernel, (4 * LANES, LANES), sides))
    packs = [pack, next_pack, last_pack]
    across = fetch(packs[1], 1)
    d_product = exchange(call(middle_kernel, (4 * LANES, LANES), product, back))
    update, d_norm, *extras = call(
        update_kernel,
        [(cells, LANES), (cells, LANES)] + [(2 * SHARE, LANES)] * MEMBERS,
        x,
        *inputs[2:],
        cot,
        w_out,
        g_out,
        o_out,
        bias_out,
        product,
        cg,
        far=10,
        scratch=[(cells, LANES), (cells, LANES), (2 * LANES, LANES), (2 * LANES, LANES)],
    )
    factors = functools.partial(
        call,
        outs=[jax.ShapeDtypeStruct((MEMBERS * cells, LANES), jnp.bfloat16)] * 2
        + [(MEMBERS * LANES, cells)],
        scratch=[(LANES, LANES), (LANES, LANES)],
    )
    prelude = (g_in, o_in, w_in, b_in)
    high, low, factor = factors(
        functools.partial(factor_kernel, (0, 1, 3)), args=(*prelude, *packs), far=7
    )
    d_product, high, low, factor, extras, across = lax.optimization_barrier(
        (d_product, high, low, factor, extras, across)
    )
    high, low, factor = factors(
        functools.partial(factor_kernel, (2,)),
        args=(*prelude, across, high, low, factor),
        far=5,
        aliases={5: 0, 6: 1, 7: 2},
    )
    extras = [extras[0]] + [hand(extras[turn], turn) for turn in range(1, MEMBERS)]
    d_sides = exchange(call(back_product_kernel, (8 * LANES, LANES), d_product, sides), PLANE)
    terms = call(weight_kernel, (6 * SHARE, LANES), d_sides, factor, high, low, *extras)
    terms, d_sides = lax.optimization_barrier((terms, d_sides))
    terms = exchange_pairs(terms, PLANE)
    cuts = call(
        cut_kernel,
        [(8 * SHARE, LANES)] * MEMBERS,
        d_sides.reshape(SHARE, 8 * MEMBERS, LANES),
    )
    terms, inputs = lax.optimization_barrier((terms, inputs))
    own = call(
        own_kernel, [(cells, LANES), (cells, LANES), (4 * LANES, cells)], *inputs, far=6, work=10**7,
    )
    cuts = [cuts[0]] + [hand(cuts[turn], turn) for turn in range(1, MEMBERS)]
    grad_pair = call(
        pair_kernel,
        (cells, LANES),
        g_in,
        w_in,
        d_norm,
        *own,
        *cuts,
        scratch=[(8 * LANES, LANES), (8 * LANES, LANES)],
        far=3,
    )
    whole = exchange_pairs(
        call(functools.partial(sum_kernel, length), (6 * LANES, LANES), terms)
    )
    d_win, d_wout = pl.pallas_call(
        last_kernel,
        out_shape=[jax.ShapeDtypeStruct(w.shape, F32) for w in (w_in, w_out)],
        in_specs=[pl.BlockSpec(memory_space=pltpu.VMEM)],
        out_specs=[pl.BlockSpec(memory_space=pltpu.HBM)] * 2,
        scratch_shapes=[pltpu.VMEM(w.shape, F32) for w in (w_in, w_out)]
        + [pltpu.SemaphoreType.DMA((6,))],
        compiler_params=pltpu.CompilerParams(vmem_limit_bytes=24 * 2**20),
    )(whole)
    return (update.reshape(pair_rep.shape), grad_pair.reshape(pair_rep.shape), d_win, d_wout)


def solution(mesh):
    whole = P(PARTS, None, None)
    placed = (whole, P(PARTS, None)) + (P(),) * 8 + (whole,)
    return jax.shard_map(
        on_device,
        mesh=jax.sharding.Mesh(mesh.devices.reshape(SIZES), PARTS),
        in_specs=placed,
        out_specs=(whole, whole, P(), P()),
        check_vma=False,
    )
```
